32 devices in a mesh: dp: 2 (over core), blk: 4 (over y, x), rep: 4 (over z).
Axes of the slice: x: 2, y: 2, z: 4, core: 2. Of those that a mesh axis runs over, the one named last changes fastest.
Arguments:
- feats: bfloat16 [2, 16384, 512], P('dp', ('blk', 'rep')), may hold values from -6 to 6
- weight: bfloat16 [512, 512], replicated, may hold values from -0.25 to 0.25
- cols: int32 [2, 128, 15], P('dp', ('blk', 'rep')), may hold values from -1 to 127, as said below
- vals: bfloat16 [2, 128, 15, 128, 128], P('dp', ('blk', 'rep')), as said below
- cotangent: bfloat16 [2, 16384, 512], P('dp', ('blk', 'rep')), may hold values from -6 to 6
Outputs:
- activ: bfloat16 [2, 16384, 512], P('dp', ('blk', 'rep'))
- feat_grad: bfloat16 [2, 16384, 512], P('dp', ('blk', 'rep'))
- weight_grad: float32 [512, 512], replicated
The draws below stay inside these ranges and needn't reach their ends.
Inputs may be any that keep to these rules, and one draw needn't show every extreme that they name: `cols`: used slots come first in each row and -1 marks the unused ones. Slot 0 of block row p names p itself; every other used slot names a block at most 7 away from p, each at most once. The relation is symmetric: p names q exactly when q names p. In every scenario some block row uses all 15 slots. `vals`: the block in row p's slot naming q is the transpose of the block in row q's slot naming p (the self block is symmetric); unused slots hold zeros.
All inputs are finite; a program needn't handle non-finite values.
Results may differ from the reference program's by a relative error of at most 0.0061.
Values may be sent and summed in bfloat16 or wider, within the bound.
No kernel may reach another device: no remote copies, remote signals or barrier semaphores. Data moves between devices by JAX's collectives and lax.ppermute only.
A program may use at most 128 MiB of HBM per device.

```python
import jax
import jax.numpy as jnp
from jax import lax

F = 512
BS = 128
REACH = 7
SLOTS = 15
SCEN = 2
NODES = 16384
NB = 128


def graph_layout(key):
    base = jax.random.fold_in(key, 101)

    def one_graph(scen):
        graph_key = jax.random.fold_in(base, scen)
        hub_key, force_key, link_key = jax.random.split(graph_key, 3)
        blocks = jnp.arange(NB, dtype=jnp.int32)
        hubs = jax.random.randint(hub_key, (NB,), 0, 16) == 0
        forced = jax.random.randint(force_key, (), REACH, NB - REACH)
        hubs = hubs | (blocks == forced)
        offsets = jnp.arange(1, REACH + 1, dtype=jnp.int32)
        upper = blocks[:, None] + offsets[None, :]
        upper_safe = jnp.clip(upper, 0, NB - 1)
        coin = jax.random.randint(link_key, (NB, REACH), 0, 100) < 28
        linked = (coin | hubs[:, None] | hubs[upper_safe]) & (upper < NB)
        lower = blocks[:, None] - offsets[None, :]
        lower_safe = jnp.clip(lower, 0, NB - 1)
        columns = jnp.arange(REACH, dtype=jnp.int32)[None, :]
        down_link = linked[lower_safe, columns] & (lower >= 0)
        valid = jnp.concatenate([jnp.ones((NB, 1), bool), linked, down_link], axis=1)
        target = jnp.concatenate([blocks[:, None], upper, lower], axis=1)
        order_key = jnp.where(valid, 0, SLOTS) + jnp.arange(SLOTS, dtype=jnp.int32)[None, :]
        order = jnp.argsort(order_key, axis=1)
        valid_sorted = jnp.take_along_axis(valid, order, axis=1)
        target_sorted = jnp.take_along_axis(target, order, axis=1)
        picked = jnp.where(valid_sorted, target_sorted, -1).astype(jnp.int32)
        counts = jnp.sum(valid.astype(jnp.int32), axis=1)
        return (picked, counts)
    return jax.vmap(one_graph)(jnp.arange(SCEN, dtype=jnp.int32))


def draw_cols(key, part):
    return graph_layout(key)[0]


def draw_vals(key, part):
    picked, counts = graph_layout(key)
    value_key = jax.random.fold_in(key, 202)
    degree = counts.astype(jnp.float32)
    scen_ids = jnp.repeat(jnp.arange(SCEN, dtype=jnp.int32), NB)
    row_ids = jnp.tile(jnp.arange(NB, dtype=jnp.int32), SCEN)

    def one_row(args):
        scen, row, row_cols = args

        def one_slot(column):
            other = jnp.maximum(column, 0)
            low = jnp.minimum(row, other)
            high = jnp.maximum(row, other)
            block_key = jax.random.fold_in(jax.random.fold_in(value_key, scen), low * NB + high)
            raw = jax.random.normal(block_key, (BS, BS), jnp.float32)
            flipped = raw.T
            block = jnp.where(row == other, (raw + flipped) * 0.70710678, jnp.where(row > other, flipped, raw))
            scale = (degree[scen, row] * degree[scen, other]) ** (-0.25) / jnp.sqrt(jnp.float32(BS))
            return jnp.where(column >= 0, block * scale, 0.0)
        return jax.vmap(one_slot)(row_cols)
    whole = lax.map(one_row, (scen_ids, row_ids, picked.reshape(SCEN * NB, SLOTS)))
    return whole.reshape(SCEN, NB, SLOTS, BS, BS).astype(jnp.bfloat16)


def block_levels(key, shape, cuts, low, largest):
    def one(axis_at, blocks):
        steps = jax.random.uniform(jax.random.fold_in(jax.random.fold_in(key, 6), axis_at), (blocks,), jnp.float32, low / len(cuts), largest / len(cuts))
        return jnp.repeat(jnp.exp(steps), shape[axis_at] // blocks).reshape((-1,) + (1,) * (len(shape) - axis_at - 1))

    level = one(*cuts[0])
    for cut in cuts[1:]:
        level = level * one(*cut)
    return level


def gaussian(own_key, shape, scale, most, pieces=(), held_as=jnp.bfloat16):
    array = jax.random.normal(own_key, shape, jnp.float32) * scale
    if len(pieces) > 0:
        array = block_levels(own_key, shape, pieces, -0.22, 0.18) * array
    return jnp.clip(array, min=-most, max=most).astype(held_as)


def setup_inputs(seed: int = 0) -> dict:
    seeds = jax.random.split(jax.random.key(seed), 6)
    feats = gaussian(seeds[0], (SCEN, NODES, F), 1.0, 6.0, ((0, 2), (1, 16)))
    weight = gaussian(seeds[1], (F, F), F ** -0.5, 0.25)
    cols = draw_cols(jax.random.fold_in(seeds[5], 71), 0)
    vals = draw_vals(jax.random.fold_in(seeds[5], 71), 0)
    cotangent = gaussian(seeds[4], (SCEN, NODES, F), 1.0, 6.0, ((0, 2), (1, 16)))
    return dict(feats=feats, weight=weight, cols=cols, vals=vals, cotangent=cotangent)


def aggregate(vals_s, cols_s, source):
    blocks = source.reshape(NB, BS, F)

    def one_row(args):
        row_vals, row_cols = args
        picked = blocks[jnp.maximum(row_cols, 0).astype(jnp.int32)]
        return jnp.einsum("kab,kbf->af", row_vals.astype(jnp.float32), picked.astype(jnp.float32))

    return lax.map(one_row, (vals_s, cols_s)).reshape(NODES, F)


def reference(feats, weight, cols, vals, cotangent):
    activ_list = []
    grad_list = []
    weight_grad = jnp.zeros((F, F), jnp.float32)
    for scen in range(SCEN):
        proj = jnp.dot(feats[scen], weight, preferred_element_type=jnp.float32).astype(jnp.bfloat16)
        agg = aggregate(vals[scen], cols[scen], proj)
        sig = jax.nn.sigmoid(agg)
        activ_list.append((agg * sig).astype(jnp.bfloat16))
        dagg = (cotangent[scen].astype(jnp.float32) * sig * (1.0 + agg * (1.0 - sig))).astype(jnp.bfloat16)
        dproj = aggregate(vals[scen], cols[scen], dagg).astype(jnp.bfloat16)
        grad_list.append(jnp.dot(dproj, weight.T, preferred_element_type=jnp.float32).astype(jnp.bfloat16))
        weight_grad = weight_grad + jnp.dot(feats[scen].T, dproj, preferred_element_type=jnp.float32)
    return jnp.stack(activ_list), jnp.stack(grad_list), weight_grad
```

```python
import functools

import jax
import jax.numpy as jnp
from jax import lax
from jax.experimental import pallas as pl
from jax.experimental.pallas import tpu as pltpu
from jax.sharding import PartitionSpec as P

REACH = 7
PAIR = 2
LINE = ("blk", "rep")
VMEM_BYTES = 40 << 20


def whole():
    return pl.BlockSpec(memory_space=pltpu.VMEM)


def held(x):
    return pltpu.with_memory_space_constraint(x, pltpu.VMEM)


def window(tile, rows):
    start = PAIR * tile
    before = REACH - start if start < REACH else 0
    own = min(rows, start + 2 * REACH + PAIR - REACH) - max(0, start - REACH)
    return start, before, own


def lanes(blocks_ref, tile, positions):
    return jnp.concatenate([blocks_ref[tile, q] for q in positions], axis=1)


def build_kernel(place_ref, vals_ref, feats_ref, band_ref, near_ref, sems):
    rows, slots = place_ref.shape
    tiles, span, height, size = band_ref.shape

    def clear(i, _):
        t, q = i // span, i % span
        band_ref[t, q] = jnp.zeros((height, size), band_ref.dtype)
        return 0

    lax.fori_loop(0, tiles * span, clear, 0)

    def copy(r, k, at):
        return pltpu.make_async_copy(
            vals_ref.at[r, k],
            band_ref.at[r // PAIR, at - PAIR * (r // PAIR), pl.ds((r % PAIR) * size, size)],
            sems.at[r, k],
        )

    for r in range(rows):
        for k in range(slots):
            at = place_ref[r, k]

            @pl.when(at >= 0)
            def _():
                copy(r, k, at).start()

    for t in range(tiles):
        for r in range(PAIR * t, PAIR * (t + 1)):
            for k in range(slots):
                at = place_ref[r, k]

                @pl.when(at >= 0)
                def _():
                    copy(r, k, at).wait()

        near_ref[pl.ds(t * height, height), :] = own_part(band_ref, t, feats_ref[...])


def own_part(band_ref, t, own):
    rows = own.shape[0] // band_ref.shape[3]
    begin = REACH - PAIR * t
    return jnp.dot(
        lanes(band_ref, t, range(begin, begin + rows)), own, preferred_element_type=jnp.float32
    )


def halo_part(band_ref, t, rows, before_ref, after_ref):
    size = band_ref.shape[3]
    span = band_ref.shape[1]
    begin = REACH - PAIR * t
    positions = [*range(begin), *range(begin + rows, span)]
    source = jnp.concatenate(
        [before_ref[PAIR * t * size :, :], after_ref[: (span - begin - rows) * size, :]], axis=0
    )
    return jnp.dot(lanes(band_ref, t, positions), source, preferred_element_type=jnp.float32)


def layer_kernel(band_ref, near_ref, before_ref, after_ref, weight_ref, cot_ref,
                 mixed_ref, activ_ref, low_ref, high_ref):
    tiles, span, height, size = band_ref.shape
    rows = tiles * PAIR
    ends = (rows - REACH) * size
    for t in range(tiles):
        at = pl.ds(t * height, height)
        mixed = near_ref[at, :] + halo_part(band_ref, t, rows, before_ref, after_ref)
        mixed = mixed.astype(jnp.bfloat16)
        mixed_ref[at, :] = mixed
        agg = jnp.dot(mixed, weight_ref[...], preferred_element_type=jnp.float32)
        sig = jax.nn.sigmoid(agg)
        activ_ref[at, :] = (agg * sig).astype(activ_ref.dtype)
        dagg = cot_ref[at, :].astype(jnp.float32) * sig * (1.0 + agg * (1.0 - sig))
        dagg = dagg.astype(jnp.bfloat16)
        skip = max(0, (t + 1) * height - low_ref.shape[0])
        low_ref[pl.ds(t * height, height - skip), :] = dagg[: height - skip]
        skip = max(0, ends - t * height)
        high_ref[pl.ds(t * height + skip - ends, height - skip), :] = dagg[skip:]


def near_kernel(band_ref, low_ref, high_ref, near_ref):
    tiles, span, height, size = band_ref.shape
    missing = tiles * height - low_ref.shape[0]
    own = jnp.concatenate([low_ref[...], high_ref[high_ref.shape[0] - missing :, :]], axis=0)
    for t in range(tiles):
        near_ref[pl.ds(t * height, height), :] = own_part(band_ref, t, own)


def back_kernel(band_ref, near_ref, before_ref, after_ref, weight_ref, out_ref):
    tiles, span, height, size = band_ref.shape
    rows = tiles * PAIR
    for t in range(tiles):
        at = pl.ds(t * height, height)
        dproj = near_ref[at, :] + halo_part(band_ref, t, rows, before_ref, after_ref)
        back = lax.dot_general(
            dproj.astype(jnp.bfloat16), weight_ref[...], (((1,), (1,)), ((), ())),
            preferred_element_type=jnp.float32,
        )
        out_ref[at, :] = back.astype(out_ref.dtype)


def kernel_call(body, outs, flops, traffic, specs, **more):
    return pl.pallas_call(
        body,
        out_shape=outs,
        in_specs=specs,
        out_specs=[whole()] * len(outs),
        compiler_params=pltpu.CompilerParams(vmem_limit_bytes=VMEM_BYTES),
        cost_estimate=pl.CostEstimate(flops=flops, bytes_accessed=traffic, transcendentals=0),
        **more,
    )


def along(x, step):
    count = lax.axis_size(LINE)
    pairs = [(i, i + step) for i in range(count) if 0 <= i + step < count]
    return lax.ppermute(x, LINE, pairs)


def partner(j, d, n):
    return j ^ d if n & (n - 1) == 0 else (j + d) % n


def scatter_sum(x, axis):
    n = lax.axis_size(axis)
    me = lax.axis_index(axis)
    step = x.shape[0] // n
    total = lax.dynamic_slice_in_dim(x, me * step, step)
    arrived = []
    for d in range(1, n):
        part = lax.dynamic_slice_in_dim(x, partner(me, d, n) * step, step)
        arrived.append(lax.ppermute(part, axis, [(j, partner(j, d, n)) for j in range(n)]))
    for part in arrived:
        total = total + part
    return total


def collect(x, axis):
    n = lax.axis_size(axis)
    me = lax.axis_index(axis)
    step = x.shape[0]
    out = jnp.zeros((n * step, x.shape[1]), x.dtype)
    out = lax.dynamic_update_slice_in_dim(out, x, me * step, 0)
    for d in range(1, n):
        part = lax.ppermute(x, axis, [(j, partner(j, d, n)) for j in range(n)])
        origin = me ^ d if n & (n - 1) == 0 else (me - d) % n
        out = lax.dynamic_update_slice_in_dim(out, part, origin * step, 0)
    return out


def shards(feats, weight, cols, vals, cotangent):
    rows, slots = cols.shape[1:]
    size = vals.shape[3]
    width = feats.shape[2]
    zones = rows * size
    tiles = rows // PAIR
    span = 2 * REACH + PAIR
    rim = REACH * size
    own = feats[0]

    before = along(own[zones - rim :], 1)
    after = along(own[:rim], -1)
    first = lax.axis_index(LINE) * rows
    place = jnp.where(cols[0] >= 0, cols[0] - first + REACH, -1)

    product = 2 * zones * zones * width
    band, near = kernel_call(
        build_kernel,
        [pltpu.VMEM((tiles, span, PAIR * size, size), jnp.bfloat16), pltpu.VMEM((zones, width), jnp.float32)],
        product, 8 << 20,
        [pl.BlockSpec(memory_space=pltpu.SMEM), pl.BlockSpec(memory_space=pl.ANY), whole()],
        scratch_shapes=[pltpu.SemaphoreType.DMA((rows, slots))],
    )(place, vals[0], own)

    mixed, activ, low, high = kernel_call(
        layer_kernel,
        [
            jax.ShapeDtypeStruct((zones, width), jnp.bfloat16),
            jax.ShapeDtypeStruct((zones, width), jnp.bfloat16),
            jax.ShapeDtypeStruct((rim, width), jnp.bfloat16),
            jax.ShapeDtypeStruct((rim, width), jnp.bfloat16),
        ],
        product * 3 // 2, 8 << 20, [whole()] * 6,
    )(held(band), held(near), before, after, weight, cotangent[0])

    before = along(high, 1)
    after = along(low, -1)
    near = kernel_call(
        near_kernel, [pltpu.VMEM((zones, width), jnp.float32)], product, 8 << 20, [whole()] * 3
    )(held(band), low, high)[0]
    dagg = jnp.concatenate([low, high[2 * rim - zones :]], axis=0)
    term = lax.dot_general(
        mixed, dagg, (((0,), (0,)), ((), ())), preferred_element_type=jnp.float32
    )
    for axis in ("dp", "blk", "rep"):
        term = scatter_sum(term, axis)
    term = term.astype(jnp.bfloat16)
    for axis in ("rep", "blk", "dp"):
        term = collect(term, axis)
    weight_grad = term.astype(jnp.float32)

    feat_grad = kernel_call(
        back_kernel, [jax.ShapeDtypeStruct((zones, width), jnp.bfloat16)],
        product * 3 // 2, 8 << 20, [whole()] * 5,
    )(held(band), held(near), before, after, weight)[0]
    return activ[None], feat_grad[None], weight_grad


def solution(mesh):
    placed = (
        P("dp", LINE, None),
        P(),
        P("dp", LINE, None),
        P("dp", LINE, None, None, None),
        P("dp", LINE, None),
    )
    return jax.shard_map(
        shards,
        mesh=mesh,
        in_specs=placed,
        out_specs=(P("dp", LINE, None), P("dp", LINE, None), P()),
        check_vma=False,
    )
```

```python
import jax
import jax.numpy as jnp
from jax import lax
from jax.experimental import pallas as pl
from jax.experimental.pallas import tpu as pltpu
from jax.sharding import PartitionSpec as P

REACH = 7
PAIR = 2
LINE = ("blk", "rep")
LEVEL = ("dp", "blk")
VMEM_BYTES = 14 << 20
BF16, F32 = jnp.bfloat16, jnp.float32


def whole():
    return pl.BlockSpec(memory_space=pltpu.VMEM)


def anywhere():
    return pl.BlockSpec(memory_space=pl.ANY)


def held(*arrays):
    return [pltpu.with_memory_space_constraint(x, pltpu.VMEM) for x in arrays]


def place():
    return lax.axis_index(LINE[0]) * lax.axis_size(LINE[1]) + lax.axis_index(LINE[1])


def is_odd():
    return lax.rem(place(), 2)


def by_parity(body):
    odd = is_odd()

    @pl.when(odd == 0)
    def _():
        body(1, 0)

    @pl.when(odd == 1)
    def _():
        body(0, 1)


def before(blocks):
    return [b - 1 for b in blocks]


def mine(blocks):
    return [REACH + b for b in blocks]


def after(blocks):
    return [2 * REACH + 1 + b for b in blocks]


def banded(band_ref, t, sources):
    size = band_ref.shape[3]
    left, right = [], []
    for indices, ref in sources:
        for i, w in enumerate(indices):
            if 0 <= w - PAIR * t < band_ref.shape[1]:
                left.append(band_ref[t, w - PAIR * t])
                right.append(ref[i * size : (i + 1) * size, :])
    return jnp.dot(
        jnp.concatenate(left, axis=1), jnp.concatenate(right, axis=0), preferred_element_type=F32
    )


def cut_kernel(feats_ref, *refs):
    outs, sems = refs[:-1], refs[-1]
    size = feats_ref.shape[0] // (REACH + 1)
    odd = is_odd()
    copies = []
    for i, (out, even_first, odd_first) in enumerate(zip(outs, (3, 0, 1, 5), (0, 3, 5, 1))):
        first = jnp.where(odd == 0, even_first, odd_first)
        source = feats_ref.at[pl.ds(pl.multiple_of(first * size, size), out.shape[0])]
        copies.append(pltpu.make_async_copy(source, out, sems.at[i]))
        copies[-1].start()
    for copy in copies:
        copy.wait()


def build_kernel(cols_ref, vals_ref, feats_ref, band_ref, near_ref, sems):
    rows, slots = cols_ref.shape
    tiles, span, height, size = band_ref.shape
    first = place() * rows - REACH

    def clear(i, _):
        band_ref[i // span, i % span] = jnp.zeros((height, size), band_ref.dtype)
        return 0

    lax.fori_loop(0, tiles * span, clear, 0)

    def each(r, act):
        for k in range(slots):
            column = cols_ref[r, k]

            @pl.when(column >= 0)
            def _():
                act(
                    pltpu.make_async_copy(
                        vals_ref.at[r, k],
                        band_ref.at[
                            r // PAIR, column - first - PAIR * (r // PAIR), pl.ds((r % PAIR) * size, size)
                        ],
                        sems.at[r, k],
                    )
                )

    for r in range(rows):
        each(r, lambda copy: copy.start())
    for t in range(tiles):
        for r in range(PAIR * t, PAIR * (t + 1)):
            each(r, lambda copy: copy.wait())
        near_ref[pl.ds(t * height, height), :] = banded(
            band_ref, t, [(mine(range(rows)), feats_ref)]
        )


def tile_step(band_ref, near_ref, sources, t, weight_ref, cot_ref):
    height = band_ref.shape[2]
    at = pl.ds(t * height, height)
    mixed = (near_ref[at, :] + banded(band_ref, t, sources)).astype(BF16)
    agg = jnp.dot(mixed, weight_ref[...], preferred_element_type=F32)
    sig = jax.nn.sigmoid(agg)
    dagg = cot_ref[at, :].astype(F32) * sig * (1.0 + agg * (1.0 - sig))
    return mixed, dagg.astype(BF16)


def inner_kernel(band_ref, near_ref, first5_ref, second5_ref, weight_ref, cot_ref,
                 mixed_ref, third_ref, fifth_ref):
    height = band_ref.shape[2]
    five = (first5_ref, second5_ref)

    def body(left, right):
        sources = [(before(range(3, 8)), five[left]), (after(range(5)), five[right])]
        for i, (t, out) in enumerate(((1, third_ref), (2, fifth_ref))):
            mixed, dagg = tile_step(band_ref, near_ref, sources, t, weight_ref, cot_ref)
            mixed_ref[pl.ds(i * height, height), :] = mixed
            out[...] = dagg

    by_parity(body)


def outer_kernel(band_ref, near_ref, first5_ref, second5_ref, first2_ref, second2_ref, weight_ref, cot_ref,
                 mixed_ref, low_ref, high_ref, first3_ref, second3_ref):
    size = band_ref.shape[3]
    height = PAIR * size
    five, two = (first5_ref, second5_ref), (first2_ref, second2_ref)
    three = (first3_ref, second3_ref)

    def body(left, right):
        sources = [
            (before(range(1, 3)), two[left]),
            (before(range(3, 8)), five[left]),
            (after(range(5)), five[right]),
            (after(range(5, 7)), two[right]),
        ]
        mixed, dagg = tile_step(band_ref, near_ref, sources, 0, weight_ref, cot_ref)
        mixed_ref[:height, :] = mixed
        low_ref[...] = dagg
        for out in three:
            out[:size, :] = dagg[size:]
        three[left][2 * size :, :] = dagg[:size]
        mixed, dagg = tile_step(band_ref, near_ref, sources, 3, weight_ref, cot_ref)
        mixed_ref[height:, :] = mixed
        high_ref[...] = dagg
        for out in three:
            out[size : 2 * size, :] = dagg[:size]
        three[right][2 * size :, :] = dagg[size:]

    by_parity(body)


def gather_kernel(band_ref, low_ref, third_ref, fifth_ref, high_ref, first_ref, second_ref,
                  mixed_mid_ref, mixed_end_ref, weight_ref, near_ref, activ_ref):
    tiles, _, height, _ = band_ref.shape
    came = (first_ref, second_ref)

    def body(left, right):
        sources = [
            (before((2, 3)), came[left]),
            (mine((0, 1)), low_ref),
            (mine((2, 3)), third_ref),
            (mine((4, 5)), fifth_ref),
            (mine((6, 7)), high_ref),
            (after((2, 3)), came[right]),
        ]
        for t in range(tiles):
            near_ref[pl.ds(t * height, height), :] = banded(band_ref, t, sources)

    by_parity(body)
    halves = (mixed_end_ref[:height, :], mixed_mid_ref[:height, :], mixed_mid_ref[height:, :], mixed_end_ref[height:, :])
    for t, mixed in enumerate(halves):
        agg = jnp.dot(mixed, weight_ref[...], preferred_element_type=F32)
        activ_ref[pl.ds(t * height, height), :] = (agg * jax.nn.sigmoid(agg)).astype(activ_ref.dtype)


def add_kernel(band_ref, near_ref, first_ref, second_ref, out_ref):
    tiles, _, height, _ = band_ref.shape
    came = (first_ref, second_ref)

    def body(left, right):
        sources = [(before((4, 5)), came[left]), (after((4, 5)), came[right])]
        for t in range(tiles):
            at = pl.ds(t * height, height)
            out_ref[at, :] = near_ref[at, :] + banded(band_ref, t, sources)

    by_parity(body)


def back_kernel(band_ref, near_ref, first3_ref, second3_ref, weight_ref, out_ref, held_ref, sems):
    tiles, _, height, _ = band_ref.shape
    came = (first3_ref, second3_ref)

    def body(left, right):
        sources = [(before((1, 6, 7)), came[left]), (after((1, 6, 0)), came[right])]
        copies = []
        for t in range(tiles):
            at = pl.ds(t * height, height)
            dproj = near_ref[at, :] + banded(band_ref, t, sources)
            held_ref[at, :] = lax.dot_general(
                dproj.astype(BF16), weight_ref[...], (((1,), (1,)), ((), ())), preferred_element_type=F32
            ).astype(BF16)
            copies.append(pltpu.make_async_copy(held_ref.at[at], out_ref.at[at], sems.at[t]))
            copies[-1].start()
        for copy in copies:
            copy.wait()

    by_parity(body)


def kernel_call(body, ins, outs, cost, specs=None, out_specs=None, **more):
    return pl.pallas_call(
        body,
        out_shape=outs,
        in_specs=specs or [whole()] * len(ins),
        out_specs=out_specs or [whole()] * len(outs),
        compiler_params=pltpu.CompilerParams(vmem_limit_bytes=VMEM_BYTES),
        cost_estimate=pl.CostEstimate(flops=cost, bytes_accessed=0, transcendentals=0),
        **more,
    )(*ins)


def swapped(first, second):
    count = lax.axis_size(LINE)
    result = []
    for x, start in ((first, 0), (second, 1)):
        pairs = [(i, i + 1) for i in range(start, count - 1, 2)]
        result.append(lax.ppermute(x, LINE, pairs + [(j, i) for i, j in pairs]))
    return result


def traded(x, axes):
    return lax.all_to_all(x.astype(BF16), axes, 0, 0, tiled=True)


def shared(x, axes):
    return traded(jnp.broadcast_to(x[None], (lax.axis_size(axes), *x.shape)), axes)


def total(parts):
    return jnp.sum(parts.astype(F32), axis=0)


def term_of(mixed, dagg):
    return lax.dot_general(mixed, dagg, (((0,), (0,)), ((), ())), preferred_element_type=F32)


def shards(feats, weight, cols, vals, cotangent):
    rows, slots = cols.shape[1:]
    size = vals.shape[3]
    width = feats.shape[2]
    zones = rows * size
    tiles = rows // PAIR
    height = PAIR * size
    span = 2 * REACH + PAIR
    own = feats[0]
    product = zones * zones * width

    def chip(blocks, dtype=BF16):
        return pltpu.VMEM((blocks * size, width), dtype)

    def plain(blocks, dtype=BF16):
        return jax.ShapeDtypeStruct((blocks * size, width), dtype)

    cut = kernel_call(
        cut_kernel, [pltpu.with_memory_space_constraint(own, pltpu.HBM)],
        [chip(5), chip(5), chip(2), chip(2)], 0, [anywhere()],
        scratch_shapes=[pltpu.SemaphoreType.DMA((4,))],
    )
    five = swapped(*cut[:2])
    two = swapped(*cut[2:])

    band, near = kernel_call(
        build_kernel, [cols[0], vals[0], own],
        [pltpu.VMEM((tiles, span, height, size), BF16), chip(rows, F32)], 4 * product,
        [pl.BlockSpec(memory_space=pltpu.SMEM), anywhere(), whole()],
        scratch_shapes=[pltpu.SemaphoreType.DMA((rows, slots))],
    )
    band, near = held(band, near)
    mixed_mid, third, fifth = kernel_call(
        inner_kernel, [band, near, *five, weight, cotangent[0]], [chip(4), chip(2), chip(2)], product
    )
    came_third = swapped(third, third)
    came_fifth = swapped(fifth, fifth)
    mixed_end, low, high, *three = kernel_call(
        outer_kernel, [band, near, *five, *two, weight, cotangent[0]],
        [chip(4), chip(2), chip(2), chip(3), chip(3)], product,
    )
    near, activ = kernel_call(
        gather_kernel, [band, low, third, fifth, high, *came_third, mixed_mid, mixed_end, weight],
        [chip(rows, F32), plain(rows)], 4 * product,
    )
    term = term_of(mixed_mid, jnp.concatenate([third, fifth])) + term_of(mixed_end, jnp.concatenate([low, high]))
    term = traded(term.reshape(lax.axis_size(LEVEL), -1, width), LEVEL)
    term, near = lax.optimization_barrier((term, near))
    term = total(term)
    term, *three = lax.optimization_barrier((term, *three))
    term = shared(term, ("rep",))
    three = swapped(*three)
    near = kernel_call(add_kernel, [band, near, *came_fifth], [chip(rows, F32)], 12 * product)[0]
    term, near = lax.optimization_barrier((term, near))
    term = shared(total(term), LEVEL)
    feat_grad = kernel_call(
        back_kernel, [band, near, *three, weight], [plain(rows)], 4 * product,
        out_specs=[anywhere()],
        scratch_shapes=[pltpu.VMEM((zones, width), BF16), pltpu.SemaphoreType.DMA((tiles,))],
    )[0]
    term, feat_grad = lax.optimization_barrier((term, feat_grad))
    weight_grad = term.reshape(-1, width).astype(F32)
    return activ[None], feat_grad[None], weight_grad


def solution(mesh):
    placed = (
        P("dp", LINE, None),
        P(),
        P("dp", LINE, None),
        P("dp", LINE, None, None, None),
        P("dp", LINE, None),
    )
    return jax.shard_map(
        shards,
        mesh=mesh,
        in_specs=placed,
        out_specs=(P("dp", LINE, None), P("dp", LINE, None), P()),
        check_vma=False,
    )
```

```python
import functools

import jax
import jax.numpy as jnp
from jax import lax
from jax.experimental import pallas as pl
from jax.experimental.pallas import tpu as pltpu
from jax.sharding import PartitionSpec as P

REACH = 7
PAIR = 2
LINE = ("blk", "rep")
LEVEL = ("dp", "blk")
VMEM_BYTES = 14 << 20
LONG = 12
BF16, F32 = jnp.bfloat16, jnp.float32


def whole():
    return pl.BlockSpec(memory_space=pltpu.VMEM)


def anywhere():
    return pl.BlockSpec(memory_space=pl.ANY)


def held(*arrays):
    return [pltpu.with_memory_space_constraint(x, pltpu.VMEM) for x in arrays]


def place():
    return lax.axis_index(LINE[0]) * lax.axis_size(LINE[1]) + lax.axis_index(LINE[1])


def is_odd():
    return lax.rem(place(), 2)


def by_parity(body):
    odd = is_odd()

    @pl.when(odd == 0)
    def _():
        body(1, 0)

    @pl.when(odd == 1)
    def _():
        body(0, 1)


def before(blocks):
    return [b - 1 for b in blocks]


def mine(blocks):
    return [REACH + b for b in blocks]


def after(blocks):
    return [2 * REACH + 1 + b for b in blocks]


def banded(band_ref, t, sources):
    size = band_ref.shape[3]
    left, right = [], []
    for indices, ref in sources:
        for i, w in enumerate(indices):
            if 0 <= w - PAIR * t < band_ref.shape[1]:
                left.append(band_ref[t, w - PAIR * t])
                right.append(ref[i * size : (i + 1) * size, :])
    return jnp.dot(
        jnp.concatenate(left, axis=1), jnp.concatenate(right, axis=0), preferred_element_type=F32
    )


def cut_kernel(feats_ref, *refs):
    outs, sems = refs[:-1], refs[-1]
    size = feats_ref.shape[0] // (REACH + 1)
    odd = is_odd()
    copies = []
    for i, (out, even_first, odd_first) in enumerate(zip(outs, (3, 0, 1, 5), (0, 3, 5, 1))):
        first = jnp.where(odd == 0, even_first, odd_first)
        source = feats_ref.at[pl.ds(pl.multiple_of(first * size, size), out.shape[0])]
        copies.append(pltpu.make_async_copy(source, out, sems.at[i]))
        copies[-1].start()
    for copy in copies:
        copy.wait()


def build_kernel(cols_ref, vals_ref, feats_ref, band_ref, near_ref, sems):
    rows, slots = cols_ref.shape
    tiles, span, height, size = band_ref.shape
    first = place() * rows - REACH

    def clear(i, _):
        band_ref[i // span, i % span] = jnp.zeros((height, size), band_ref.dtype)
        return 0

    lax.fori_loop(0, tiles * span, clear, 0)

    def each(r, act):
        for k in range(slots):
            column = cols_ref[r, k]

            @pl.when(column >= 0)
            def _():
                act(
                    pltpu.make_async_copy(
                        vals_ref.at[r, k],
                        band_ref.at[
                            r // PAIR, column - first - PAIR * (r // PAIR), pl.ds((r % PAIR) * size, size)
                        ],
                        sems.at[r, k],
                    )
                )

    for r in range(rows):
        each(r, lambda copy: copy.start())
    for t in range(tiles):
        for r in range(PAIR * t, PAIR * (t + 1)):
            each(r, lambda copy: copy.wait())
        near_ref[pl.ds(t * height, height), :] = banded(
            band_ref, t, [(mine(range(rows)), feats_ref)]
        )


def tile_step(band_ref, near_ref, sources, t, weight_ref, cot_ref):
    height = band_ref.shape[2]
    at = pl.ds(t * height, height)
    mixed = (near_ref[at, :] + banded(band_ref, t, sources)).astype(BF16)
    agg = jnp.dot(mixed, weight_ref[...], preferred_element_type=F32)
    sig = jax.nn.sigmoid(agg)
    dagg = cot_ref[at, :].astype(F32) * sig * (1.0 + agg * (1.0 - sig))
    return mixed, dagg.astype(BF16)


def inner_kernel(band_ref, near_ref, first5_ref, second5_ref, weight_ref, cot_ref, mixed_ref, mid_ref):
    height = band_ref.shape[2]
    five = (first5_ref, second5_ref)

    def body(left, right):
        sources = [(before(range(3, 8)), five[left]), (after(range(5)), five[right])]
        for i, t in enumerate((1, 2)):
            mixed, dagg = tile_step(band_ref, near_ref, sources, t, weight_ref, cot_ref)
            at = pl.ds(i * height, height)
            mixed_ref[at, :] = mixed
            mid_ref[at, :] = dagg

    by_parity(body)


def outer_kernel(band_ref, near_ref, first5_ref, second5_ref, first2_ref, second2_ref, weight_ref, cot_ref, mid_ref,
                 mixed_ref, end_ref, first3_ref, second3_ref, all7_ref):
    size = band_ref.shape[3]
    height = PAIR * size
    five, two = (first5_ref, second5_ref), (first2_ref, second2_ref)
    three = (first3_ref, second3_ref)

    def body(left, right):
        sources = [
            (before(range(1, 3)), two[left]),
            (before(range(3, 8)), five[left]),
            (after(range(5)), five[right]),
            (after(range(5, 7)), two[right]),
        ]
        mixed, dagg = tile_step(band_ref, near_ref, sources, 0, weight_ref, cot_ref)
        mixed_ref[:height, :] = mixed
        end_ref[:height, :] = dagg
        for out in three:
            out[:size, :] = dagg[size:]
        three[left][2 * size :, :] = dagg[:size]
        mixed, dagg = tile_step(band_ref, near_ref, sources, 3, weight_ref, cot_ref)
        mixed_ref[height:, :] = mixed
        end_ref[height:, :] = dagg
        for out in three:
            out[size : 2 * size, :] = dagg[:size]
        three[right][2 * size :, :] = dagg[size:]
        all7_ref[: 4 * size, :] = mid_ref[...]
        all7_ref[4 * size :, :] = second3_ref[...]

    by_parity(body)


def own_kernel(band_ref, mid_ref, end_ref, near_ref):
    tiles, _, height, _ = band_ref.shape
    sources = [
        (mine((0, 1)), end_ref.at[:height]),
        (mine((2, 3, 4, 5)), mid_ref),
        (mine((6, 7)), end_ref.at[height:]),
    ]
    for t in range(tiles):
        near_ref[pl.ds(t * height, height), :] = banded(band_ref, t, sources)


def mark_kernel(near_ref, out_ref):
    out_ref[...] = near_ref[: out_ref.shape[0], : out_ref.shape[1]]


def activ_kernel(mixed_mid_ref, mixed_end_ref, weight_ref, _, activ_ref):
    height = mixed_mid_ref.shape[0] // 2
    halves = (mixed_end_ref[:height, :], mixed_mid_ref[:height, :], mixed_mid_ref[height:, :], mixed_end_ref[height:, :])
    for t, mixed in enumerate(halves):
        agg = jnp.dot(mixed, weight_ref[...], preferred_element_type=F32)
        activ_ref[pl.ds(t * height, height), :] = (agg * jax.nn.sigmoid(agg)).astype(activ_ref.dtype)


def add_kernel(left_rows, right_rows, band_ref, near_ref, first_ref, second_ref, out_ref):
    tiles, _, height, _ = band_ref.shape
    came = (first_ref, second_ref)

    def body(left, right):
        sources = [(before(left_rows), came[left]), (after(right_rows), came[right])]
        for t in range(tiles):
            at = pl.ds(t * height, height)
            out_ref[at, :] = near_ref[at, :] + banded(band_ref, t, sources)

    by_parity(body)


def back_kernel(band_ref, near_ref, all7_ref, weight_ref, out_ref, held_ref, sems):
    tiles, _, height, _ = band_ref.shape

    def body(left, right):
        if left:
            sources = [(before((2, 3, 4, 5, 1, 6, 7)), all7_ref)]
        else:
            sources = [(after((2, 3, 4, 5, 1, 6, 0)), all7_ref)]
        copies = []
        for t in range(tiles):
            at = pl.ds(t * height, height)
            dproj = near_ref[at, :] + banded(band_ref, t, sources)
            held_ref[at, :] = lax.dot_general(
                dproj.astype(BF16), weight_ref[...], (((1,), (1,)), ((), ())), preferred_element_type=F32
            ).astype(BF16)
            copies.append(pltpu.make_async_copy(held_ref.at[at], out_ref.at[at], sems.at[t]))
            copies[-1].start()
        for copy in copies:
            copy.wait()

    by_parity(body)


def kernel_call(body, ins, outs, cost, specs=None, out_specs=None, **more):
    return pl.pallas_call(
        body,
        out_shape=outs,
        in_specs=specs or [whole()] * len(ins),
        out_specs=out_specs or [whole()] * len(outs),
        compiler_params=pltpu.CompilerParams(vmem_limit_bytes=VMEM_BYTES),
        cost_estimate=pl.CostEstimate(flops=cost, bytes_accessed=0, transcendentals=0),
        **more,
    )(*ins)


def swap_pairs(start, across):
    count, run = lax.axis_size(LINE), lax.axis_size(LINE[1])
    pairs = [(i, i + 1) for i in range(start, count - 1, 2)]
    pairs = [(i, j) for i, j in pairs if across is None or (j % run == 0) == across]
    return pairs + [(j, i) for i, j in pairs]


def swapped(first, second, across=None):
    return [lax.ppermute(x, LINE, swap_pairs(start, across)) for x, start in ((first, 0), (second, 1))]


def partner(j, d, n):
    return j ^ d if n & (n - 1) == 0 else (j + d) % n


def from_all(parts, axis):
    n = lax.axis_size(axis)
    return [
        lax.ppermute(parts(d), axis, [(j, partner(j, d, n)) for j in range(n)]) for d in range(1, n)
    ]


def scatter(x, axis, dtype):
    n = lax.axis_size(axis)
    me = lax.axis_index(axis)
    step = x.shape[0] // n

    def part(d):
        return lax.dynamic_slice_in_dim(x, partner(me, d, n) * step, step)

    return part(0) if n & (n - 1) == 0 else lax.dynamic_slice_in_dim(x, me * step, step), from_all(
        lambda d: part(d).astype(dtype), axis
    )


def add_all(kept, came):
    for part in came:
        kept = kept + part.astype(F32)
    return kept


def pairwise(parts):
    parts = [part.astype(F32) for part in parts]
    while len(parts) > 1:
        parts = [parts[i] + parts[i + 1] for i in range(0, len(parts), 2)]
    return parts[0]


def join_kernel(*refs):
    *parts, out_ref = refs
    n = lax.axis_size(LEVEL[1])
    me = lax.axis_index(LEVEL[1])
    halves = lax.axis_size(LEVEL[0])
    step = parts[0].shape[0] // halves
    for d, part in enumerate(parts):
        origin = me ^ d if n & (n - 1) == 0 else lax.rem(me - d + n, n)
        for h in range(halves):
            first = pl.multiple_of(h * n * step + origin * step, step)
            out_ref[pl.ds(first, step), :] = part[h * step : (h + 1) * step, :].astype(out_ref.dtype)


def term_of(mixed, dagg):
    return lax.dot_general(mixed, dagg, (((0,), (0,)), ((), ())), preferred_element_type=F32)


def shards(feats, weight, cols, vals, cotangent):
    rows, slots = cols.shape[1:]
    size = vals.shape[3]
    width = feats.shape[2]
    zones = rows * size
    tiles = rows // PAIR
    height = PAIR * size
    span = 2 * REACH + PAIR
    own = feats[0]
    product = zones * zones * width

    def chip(blocks, dtype=BF16):
        return pltpu.VMEM((blocks * size, width), dtype)

    def plain(blocks, dtype=BF16):
        return jax.ShapeDtypeStruct((blocks * size, width), dtype)

    cut = kernel_call(
        cut_kernel, [pltpu.with_memory_space_constraint(own, pltpu.HBM)],
        [chip(5), chip(5), chip(2), chip(2)], 0, [anywhere()],
        scratch_shapes=[pltpu.SemaphoreType.DMA((4,))],
    )
    five = swapped(*cut[:2])
    two = swapped(*cut[2:])

    band, near = kernel_call(
        build_kernel, [cols[0], vals[0], own],
        [pltpu.VMEM((tiles, span, height, size), BF16), chip(rows, F32)], 4 * product,
        [pl.BlockSpec(memory_space=pltpu.SMEM), anywhere(), whole()],
        scratch_shapes=[pltpu.SemaphoreType.DMA((rows, slots))],
    )
    band, near = held(band, near)
    mixed_mid, mid = kernel_call(
        inner_kernel, [band, near, *five, weight, cotangent[0]], [chip(4), chip(4)], product
    )
    four = swapped(mid, mid, across=False)
    mixed_end, end, *three, all7 = kernel_call(
        outer_kernel, [band, near, *five, *two, weight, cotangent[0], mid],
        [chip(4), chip(4), chip(3), chip(3), chip(7)], product,
    )
    three = swapped(*three, across=False)
    full = [chip(rows, F32)]
    term = term_of(mixed_mid, mid) + term_of(mixed_end, end)
    kept, came = scatter(term, LEVEL[0], F32)
    near = kernel_call(own_kernel, [band, mid, end], full, LONG * product)[0]
    came, near = lax.optimization_barrier((came, near))
    kept, came = scatter(add_all(kept, came), LEVEL[1], BF16)
    near = kernel_call(
        functools.partial(add_kernel, (2, 3, 4, 5), (2, 3, 4, 5)), [band, *held(near), *four], full, LONG * product
    )[0]
    came, near = lax.optimization_barrier((came, near))
    term = add_all(kept, came).astype(BF16)
    parts = [term, *from_all(lambda d: term, "rep")]
    mark = kernel_call(mark_kernel, held(near), [pltpu.VMEM((8, 128), F32)], LONG * product)[0]
    *parts, all7, mark = lax.optimization_barrier((*parts, all7, mark))
    all7 = lax.ppermute(all7, LINE, swap_pairs(1, True))
    term = pairwise(parts).astype(BF16)
    other, = from_all(lambda d: term, LEVEL[0])
    activ = kernel_call(
        activ_kernel, [mixed_mid, mixed_end, weight, *held(mark)], [plain(rows)], LONG * product
    )[0]
    other, activ = lax.optimization_barrier((other, activ))
    term = jnp.where(lax.axis_index(LEVEL[0]) == 0, jnp.stack([term, other]), jnp.stack([other, term]))
    term = term.reshape(-1, width)
    parts = [term, *from_all(lambda d: term, LEVEL[1])]
    near = kernel_call(
        functools.partial(add_kernel, (1, 6, 7), (1, 6, 0)), [band, *held(near), *three], full, LONG * product
    )[0]
    parts, near = lax.optimization_barrier((parts, near))
    feat_grad = kernel_call(
        back_kernel, [band, *held(near), all7, weight], [plain(rows)], LONG * product,
        out_specs=[anywhere()],
        scratch_shapes=[pltpu.VMEM((zones, width), BF16), pltpu.SemaphoreType.DMA((tiles,))],
    )[0]
    parts, feat_grad = lax.optimization_barrier((parts, feat_grad))
    weight_grad = kernel_call(
        join_kernel, parts, [jax.ShapeDtypeStruct((width, width), F32)], 0
    )[0]
    return activ[None], feat_grad[None], weight_grad


def solution(mesh):
    placed = (
        P("dp", LINE, None),
        P(),
        P("dp", LINE, None),
        P("dp", LINE, None, None, None),
        P("dp", LINE, None),
    )
    return jax.shard_map(
        shards,
        mesh=mesh,
        in_specs=placed,
        out_specs=(P("dp", LINE, None), P("dp", LINE, None), P()),
        check_vma=False,
    )
```

```python
import jax
import jax.numpy as jnp
from jax import lax
from jax.experimental import pallas as pl
from jax.experimental.pallas import tpu as pltpu
from jax.sharding import PartitionSpec as P

REACH = 7
PAIR = 2
LINE = ("blk", "rep")
LEVEL = ("dp", "blk")
VMEM_BYTES = 14 << 20
BF16, F32 = jnp.bfloat16, jnp.float32


def whole():
    return pl.BlockSpec(memory_space=pltpu.VMEM)


def anywhere():
    return pl.BlockSpec(memory_space=pl.ANY)


def held(*arrays):
    return [pltpu.with_memory_space_constraint(x, pltpu.VMEM) for x in arrays]


def place():
    return lax.axis_index(LINE[0]) * lax.axis_size(LINE[1]) + lax.axis_index(LINE[1])


def is_odd():
    return lax.rem(place(), 2)


def by_parity(body):
    odd = is_odd()

    @pl.when(odd == 0)
    def _():
        body(1, 0)

    @pl.when(odd == 1)
    def _():
        body(0, 1)


def before(blocks):
    return [b - 1 for b in blocks]


def mine(blocks):
    return [REACH + b for b in blocks]


def after(blocks):
    return [2 * REACH + 1 + b for b in blocks]


def banded(band_ref, t, sources):
    size = band_ref.shape[3]
    left, right = [], []
    for indices, ref in sources:
        for i, w in enumerate(indices):
            if 0 <= w - PAIR * t < band_ref.shape[1]:
                left.append(band_ref[t, w - PAIR * t])
                right.append(ref[i * size : (i + 1) * size, :])
    return jnp.dot(
        jnp.concatenate(left, axis=1), jnp.concatenate(right, axis=0), preferred_element_type=F32
    )


def cut_kernel(feats_ref, *refs):
    outs, sems = refs[:-1], refs[-1]
    size = feats_ref.shape[0] // (REACH + 1)
    odd = is_odd()
    copies = []
    for i, (out, even_first, odd_first) in enumerate(zip(outs, (3, 0, 1, 5), (0, 3, 5, 1))):
        first = jnp.where(odd == 0, even_first, odd_first)
        source = feats_ref.at[pl.ds(pl.multiple_of(first * size, size), out.shape[0])]
        copies.append(pltpu.make_async_copy(source, out, sems.at[i]))
        copies[-1].start()
    for copy in copies:
        copy.wait()


def build_kernel(cols_ref, vals_ref, feats_ref, band_ref, near_ref, sems):
    rows, slots = cols_ref.shape
    tiles, span, height, size = band_ref.shape
    first = place() * rows - REACH

    def clear(i, _):
        band_ref[i // span, i % span] = jnp.zeros((height, size), band_ref.dtype)
        return 0

    lax.fori_loop(0, tiles * span, clear, 0)

    def each(r, act):
        for k in range(slots):
            column = cols_ref[r, k]

            @pl.when(column >= 0)
            def _():
                act(
                    pltpu.make_async_copy(
                        vals_ref.at[r, k],
                        band_ref.at[
                            r // PAIR, column - first - PAIR * (r // PAIR), pl.ds((r % PAIR) * size, size)
                        ],
                        sems.at[r, k],
                    )
                )

    for r in range(rows):
        each(r, lambda copy: copy.start())
    for t in range(tiles):
        for r in range(PAIR * t, PAIR * (t + 1)):
            each(r, lambda copy: copy.wait())
        near_ref[pl.ds(t * height, height), :] = banded(
            band_ref, t, [(mine(range(rows)), feats_ref)]
        )


def tile_step(band_ref, near_ref, sources, t, weight_ref, cot_ref):
    height = band_ref.shape[2]
    at = pl.ds(t * height, height)
    mixed = (near_ref[at, :] + banded(band_ref, t, sources)).astype(BF16)
    agg = jnp.dot(mixed, weight_ref[...], preferred_element_type=F32)
    sig = jax.nn.sigmoid(agg)
    dagg = cot_ref[at, :].astype(F32) * sig * (1.0 + agg * (1.0 - sig))
    return mixed, dagg.astype(BF16)


def inner_kernel(band_ref, near_ref, first5_ref, second5_ref, weight_ref, cot_ref, mixed_ref, mid_ref):
    height = band_ref.shape[2]
    five = (first5_ref, second5_ref)

    def body(left, right):
        sources = [(before(range(3, 8)), five[left]), (after(range(5)), five[right])]
        for i, t in enumerate((1, 2)):
            mixed, dagg = tile_step(band_ref, near_ref, sources, t, weight_ref, cot_ref)
            at = pl.ds(i * height, height)
            mixed_ref[at, :] = mixed
            mid_ref[at, :] = dagg

    by_parity(body)


def outer_kernel(band_ref, near_ref, first5_ref, second5_ref, first2_ref, second2_ref, weight_ref, cot_ref,
                 mixed_ref, end_ref, first3_ref, second3_ref):
    size = band_ref.shape[3]
    height = PAIR * size
    five, two = (first5_ref, second5_ref), (first2_ref, second2_ref)
    three = (first3_ref, second3_ref)

    def body(left, right):
        sources = [
            (before(range(1, 3)), two[left]),
            (before(range(3, 8)), five[left]),
            (after(range(5)), five[right]),
            (after(range(5, 7)), two[right]),
        ]
        mixed, dagg = tile_step(band_ref, near_ref, sources, 0, weight_ref, cot_ref)
        mixed_ref[:height, :] = mixed
        end_ref[:height, :] = dagg
        for out in three:
            out[:size, :] = dagg[size:]
        three[left][2 * size :, :] = dagg[:size]
        mixed, dagg = tile_step(band_ref, near_ref, sources, 3, weight_ref, cot_ref)
        mixed_ref[height:, :] = mixed
        end_ref[height:, :] = dagg
        for out in three:
            out[size : 2 * size, :] = dagg[:size]
        three[right][2 * size :, :] = dagg[size:]

    by_parity(body)


def own_kernel(band_ref, mid_ref, end_ref, mixed_mid_ref, mixed_end_ref, weight_ref, near_ref, activ_ref):
    tiles, _, height, _ = band_ref.shape
    sources = [
        (mine((0, 1)), end_ref.at[:height]),
        (mine((2, 3, 4, 5)), mid_ref),
        (mine((6, 7)), end_ref.at[height:]),
    ]
    halves = (mixed_end_ref[:height, :], mixed_mid_ref[:height, :], mixed_mid_ref[height:, :], mixed_end_ref[height:, :])
    for t, mixed in enumerate(halves):
        at = pl.ds(t * height, height)
        near_ref[at, :] = banded(band_ref, t, sources)
        agg = jnp.dot(mixed, weight_ref[...], preferred_element_type=F32)
        activ_ref[at, :] = (agg * jax.nn.sigmoid(agg)).astype(activ_ref.dtype)


LAST = before((1, 6, 7)) + after((1, 6, 0))


def last_of(t, span):
    return [i for i, w in enumerate(LAST) if 0 <= w - PAIR * t < span]


def add_kernel(band_ref, near_ref, first4_ref, second4_ref, out_ref, last_ref):
    tiles, span, height, _ = band_ref.shape
    for t in range(tiles):
        for i, which in enumerate(last_of(t, span)):
            last_ref[t, i] = band_ref[t, LAST[which] - PAIR * t]
    four = (first4_ref, second4_ref)

    def body(left, right):
        sources = [(before(range(2, 6)), four[left]), (after(range(2, 6)), four[right])]
        for t in range(tiles):
            at = pl.ds(t * height, height)
            out_ref[at, :] = near_ref[at, :] + banded(band_ref, t, sources)

    by_parity(body)


def back_kernel(last_ref, near_ref, first3_ref, second3_ref, weight_ref, out_ref, held_ref, sems):
    tiles, _, height, size = last_ref.shape
    three = (first3_ref, second3_ref)

    def body(left, right):
        sources = [(side, i * size) for side in (left, right) for i in range(3)]
        copies = []
        for t in range(tiles):
            at = pl.ds(t * height, height)
            met = last_of(t, 2 * REACH + PAIR)
            blocks = [three[side][first : first + size, :] for side, first in (sources[i] for i in met)]
            dproj = near_ref[at, :] + jnp.dot(
                jnp.concatenate([last_ref[t, i] for i in range(len(met))], axis=1),
                jnp.concatenate(blocks, axis=0),
                preferred_element_type=F32,
            )
            held_ref[at, :] = lax.dot_general(
                dproj.astype(BF16), weight_ref[...], (((1,), (1,)), ((), ())), preferred_element_type=F32
            ).astype(BF16)
            copies.append(pltpu.make_async_copy(held_ref.at[at], out_ref.at[at], sems.at[t]))
            copies[-1].start()
        for copy in copies:
            copy.wait()

    by_parity(body)


def kernel_call(body, ins, outs, cost, specs=None, out_specs=None, **more):
    return pl.pallas_call(
        body,
        out_shape=outs,
        in_specs=specs or [whole()] * len(ins),
        out_specs=out_specs or [whole()] * len(outs),
        compiler_params=pltpu.CompilerParams(vmem_limit_bytes=VMEM_BYTES),
        cost_estimate=pl.CostEstimate(flops=cost, bytes_accessed=0, transcendentals=0),
        **more,
    )(*ins)


def swapped(first, second):
    count = lax.axis_size(LINE)
    result = []
    for x, start in ((first, 0), (second, 1)):
        pairs = [(i, i + 1) for i in range(start, count - 1, 2)]
        result.append(lax.ppermute(x, LINE, pairs + [(j, i) for i, j in pairs]))
    return result


def partner(j, d, n):
    return j ^ d if n & (n - 1) == 0 else (j + d) % n


def from_all(parts, axis):
    n = lax.axis_size(axis)
    return [
        lax.ppermute(parts(d), axis, [(j, partner(j, d, n)) for j in range(n)]) for d in range(1, n)
    ]


def pairwise(parts):
    parts = [part.astype(F32) for part in parts]
    while len(parts) > 1:
        parts = [parts[i] + parts[i + 1] for i in range(0, len(parts), 2)]
    return parts[0]


def join_kernel(*refs):
    *parts, out_ref = refs
    n = lax.axis_size(LEVEL[1])
    me = lax.axis_index(LEVEL[1])
    halves = lax.axis_size(LEVEL[0])
    step = parts[0].shape[0] // halves
    for d, part in enumerate(parts):
        origin = me ^ d if n & (n - 1) == 0 else lax.rem(me - d + n, n)
        for h in range(halves):
            first = pl.multiple_of(h * n * step + origin * step, step)
            out_ref[pl.ds(first, step), :] = part[h * step : (h + 1) * step, :].astype(out_ref.dtype)


def term_of(mixed, dagg):
    return lax.dot_general(mixed, dagg, (((0,), (0,)), ((), ())), preferred_element_type=F32)


def shards(feats, weight, cols, vals, cotangent):
    rows, slots = cols.shape[1:]
    size = vals.shape[3]
    width = feats.shape[2]
    zones = rows * size
    tiles = rows // PAIR
    height = PAIR * size
    span = 2 * REACH + PAIR
    own = feats[0]
    product = zones * zones * width

    def chip(blocks, dtype=BF16):
        return pltpu.VMEM((blocks * size, width), dtype)

    def plain(blocks, dtype=BF16):
        return jax.ShapeDtypeStruct((blocks * size, width), dtype)

    cut = kernel_call(
        cut_kernel, [pltpu.with_memory_space_constraint(own, pltpu.HBM)],
        [chip(5), chip(5), chip(2), chip(2)], 0, [anywhere()],
        scratch_shapes=[pltpu.SemaphoreType.DMA((4,))],
    )
    five = swapped(*cut[:2])
    two = swapped(*cut[2:])

    band, near = kernel_call(
        build_kernel, [cols[0], vals[0], own],
        [pltpu.VMEM((tiles, span, height, size), BF16), chip(rows, F32)], 4 * product,
        [pl.BlockSpec(memory_space=pltpu.SMEM), anywhere(), whole()],
        scratch_shapes=[pltpu.SemaphoreType.DMA((rows, slots))],
    )
    band, near = held(band, near)
    mixed_mid, mid = kernel_call(
        inner_kernel, [band, near, *five, weight, cotangent[0]], [chip(4), chip(4)], product
    )
    four = swapped(mid, mid)
    mixed_end, end, *sent = kernel_call(
        outer_kernel, [band, near, *five, *two, weight, cotangent[0]],
        [chip(4), chip(4), chip(3), chip(3)], product,
    )
    three = swapped(*sent)
    near, activ = kernel_call(
        own_kernel, [band, mid, end, mixed_mid, mixed_end, weight], [chip(rows, F32), plain(rows)], product
    )
    near, last = kernel_call(
        add_kernel, [band, held(near)[0], *four],
        [chip(rows, F32), pltpu.VMEM((tiles, len(last_of(0, span)), height, size), BF16)], 12 * product,
    )
    term = term_of(mixed_mid, mid) + term_of(mixed_end, end)
    term = lax.all_to_all(
        term.astype(BF16).reshape(lax.axis_size(LEVEL), -1, width), LEVEL, 0, 0, tiled=True
    )
    term, near = lax.optimization_barrier((term, near))
    term = jnp.sum(term.astype(F32), axis=0)
    term = term.astype(BF16)
    parts = [term, *from_all(lambda d: term, "rep")]
    feat_grad = kernel_call(
        back_kernel, [*held(last, near), *three, weight], [plain(rows)], 12 * product,
        out_specs=[anywhere()],
        scratch_shapes=[pltpu.VMEM((zones, width), BF16), pltpu.SemaphoreType.DMA((tiles,))],
    )[0]
    parts, feat_grad = lax.optimization_barrier((parts, feat_grad))
    term = pairwise(parts).astype(BF16)
    other, = from_all(lambda d: term, LEVEL[0])
    term = jnp.where(lax.axis_index(LEVEL[0]) == 0, jnp.stack([term, other]), jnp.stack([other, term]))
    term = term.reshape(-1, width)
    parts = [term, *from_all(lambda d: term, LEVEL[1])]
    weight_grad = kernel_call(
        join_kernel, parts, [jax.ShapeDtypeStruct((width, width), F32)], 0
    )[0]
    return activ[None], feat_grad[None], weight_grad


def solution(mesh):
    placed = (
        P("dp", LINE, None),
        P(),
        P("dp", LINE, None),
        P("dp", LINE, None, None, None),
        P("dp", LINE, None),
    )
    return jax.shard_map(
        shards,
        mesh=mesh,
        in_specs=placed,
        out_specs=(P("dp", LINE, None), P("dp", LINE, None), P()),
        check_vma=False,
    )
```

```python
import functools

import jax
import jax.numpy as jnp
from jax import lax
from jax.experimental import pallas as pl
from jax.experimental.pallas import tpu as pltpu
from jax.sharding import PartitionSpec as P

REACH = 7
PAIR = 2
LINE = ("blk", "rep")
LEVEL = ("dp", "blk")
VMEM_BYTES = 14 << 20
LONG = 12
BF16, F32 = jnp.bfloat16, jnp.float32


def whole():
    return pl.BlockSpec(memory_space=pltpu.VMEM)


def anywhere():
    return pl.BlockSpec(memory_space=pl.ANY)


def held(*arrays):
    return [pltpu.with_memory_space_constraint(x, pltpu.VMEM) for x in arrays]


def place():
    return lax.axis_index(LINE[0]) * lax.axis_size(LINE[1]) + lax.axis_index(LINE[1])


def is_odd():
    return lax.rem(place(), 2)


def by_parity(body):
    odd = is_odd()

    @pl.when(odd == 0)
    def _():
        body(1, 0)

    @pl.when(odd == 1)
    def _():
        body(0, 1)


def before(blocks):
    return [b - 1 for b in blocks]


def mine(blocks):
    return [REACH + b for b in blocks]


def after(blocks):
    return [2 * REACH + 1 + b for b in blocks]


def banded(band_ref, t, sources):
    size = band_ref.shape[3]
    left, right = [], []
    for indices, ref in sources:
        for i, w in enumerate(indices):
            if 0 <= w - PAIR * t < band_ref.shape[1]:
                left.append(band_ref[t, w - PAIR * t])
                right.append(ref[i * size : (i + 1) * size, :])
    return jnp.dot(
        jnp.concatenate(left, axis=1), jnp.concatenate(right, axis=0), preferred_element_type=F32
    )


def cut_kernel(feats_ref, *refs):
    outs, sems = refs[:-1], refs[-1]
    size = feats_ref.shape[0] // (REACH + 1)
    odd = is_odd()
    copies = []
    for i, (out, even_first, odd_first) in enumerate(zip(outs, (3, 0, 1, 5), (0, 3, 5, 1))):
        first = jnp.where(odd == 0, even_first, odd_first)
        source = feats_ref.at[pl.ds(pl.multiple_of(first * size, size), out.shape[0])]
        copies.append(pltpu.make_async_copy(source, out, sems.at[i]))
        copies[-1].start()
    for copy in copies:
        copy.wait()


def build_kernel(cols_ref, vals_ref, feats_ref, band_ref, near_ref, sems):
    rows, slots = cols_ref.shape
    tiles, span, height, size = band_ref.shape
    first = place() * rows - REACH

    def clear(i, _):
        band_ref[i // span, i % span] = jnp.zeros((height, size), band_ref.dtype)
        return 0

    lax.fori_loop(0, tiles * span, clear, 0)

    def each(r, act):
        for k in range(slots):
            column = cols_ref[r, k]

            @pl.when(column >= 0)
            def _():
                act(
                    pltpu.make_async_copy(
                        vals_ref.at[r, k],
                        band_ref.at[
                            r // PAIR, column - first - PAIR * (r // PAIR), pl.ds((r % PAIR) * size, size)
                        ],
                        sems.at[r, k],
                    )
                )

    for r in range(rows):
        each(r, lambda copy: copy.start())
    for t in range(tiles):
        for r in range(PAIR * t, PAIR * (t + 1)):
            each(r, lambda copy: copy.wait())
        near_ref[pl.ds(t * height, height), :] = banded(
            band_ref, t, [(mine(range(rows)), feats_ref)]
        )


def tile_step(band_ref, near_ref, sources, t, weight_ref, cot_ref):
    height = band_ref.shape[2]
    at = pl.ds(t * height, height)
    mixed = (near_ref[at, :] + banded(band_ref, t, sources)).astype(BF16)
    agg = jnp.dot(mixed, weight_ref[...], preferred_element_type=F32)
    sig = jax.nn.sigmoid(agg)
    dagg = cot_ref[at, :].astype(F32) * sig * (1.0 + agg * (1.0 - sig))
    return mixed, dagg.astype(BF16)


def inner_kernel(band_ref, near_ref, first5_ref, second5_ref, weight_ref, cot_ref, mixed_ref, mid_ref):
    height = band_ref.shape[2]
    five = (first5_ref, second5_ref)

    def body(left, right):
        sources = [(before(range(3, 8)), five[left]), (after(range(5)), five[right])]
        for i, t in enumerate((1, 2)):
            mixed, dagg = tile_step(band_ref, near_ref, sources, t, weight_ref, cot_ref)
            at = pl.ds(i * height, height)
            mixed_ref[at, :] = mixed
            mid_ref[at, :] = dagg

    by_parity(body)


def outer_kernel(band_ref, near_ref, first5_ref, second5_ref, first2_ref, second2_ref, weight_ref, cot_ref,
                 mixed_ref, end_ref, first3_ref, second3_ref):
    size = band_ref.shape[3]
    height = PAIR * size
    five, two = (first5_ref, second5_ref), (first2_ref, second2_ref)
    three = (first3_ref, second3_ref)

    def body(left, right):
        sources = [
            (before(range(1, 3)), two[left]),
            (before(range(3, 8)), five[left]),
            (after(range(5)), five[right]),
            (after(range(5, 7)), two[right]),
        ]
        mixed, dagg = tile_step(band_ref, near_ref, sources, 0, weight_ref, cot_ref)
        mixed_ref[:height, :] = mixed
        end_ref[:height, :] = dagg
        for out in three:
            out[:size, :] = dagg[size:]
        three[left][2 * size :, :] = dagg[:size]
        mixed, dagg = tile_step(band_ref, near_ref, sources, 3, weight_ref, cot_ref)
        mixed_ref[height:, :] = mixed
        end_ref[height:, :] = dagg
        for out in three:
            out[size : 2 * size, :] = dagg[:size]
        three[right][2 * size :, :] = dagg[size:]

    by_parity(body)


def own_kernel(band_ref, mid_ref, end_ref, mixed_mid_ref, mixed_end_ref, weight_ref, near_ref, activ_ref):
    tiles, _, height, _ = band_ref.shape
    sources = [
        (mine((0, 1)), end_ref.at[:height]),
        (mine((2, 3, 4, 5)), mid_ref),
        (mine((6, 7)), end_ref.at[height:]),
    ]
    halves = (mixed_end_ref[:height, :], mixed_mid_ref[:height, :], mixed_mid_ref[height:, :], mixed_end_ref[height:, :])
    for t, mixed in enumerate(halves):
        at = pl.ds(t * height, height)
        near_ref[at, :] = banded(band_ref, t, sources)
        agg = jnp.dot(mixed, weight_ref[...], preferred_element_type=F32)
        activ_ref[at, :] = (agg * jax.nn.sigmoid(agg)).astype(activ_ref.dtype)


def mark_kernel(near_ref, out_ref):
    out_ref[...] = near_ref[: out_ref.shape[0], : out_ref.shape[1]]


def add_kernel(left_rows, right_rows, band_ref, near_ref, first_ref, second_ref, out_ref):
    tiles, _, height, _ = band_ref.shape
    came = (first_ref, second_ref)

    def body(left, right):
        sources = [(before(left_rows), came[left]), (after(right_rows), came[right])]
        for t in range(tiles):
            at = pl.ds(t * height, height)
            out_ref[at, :] = near_ref[at, :] + banded(band_ref, t, sources)

    by_parity(body)


def back_kernel(band_ref, near_ref, first3_ref, second3_ref, weight_ref, _, out_ref, held_ref, sems):
    tiles, _, height, _ = band_ref.shape
    three = (first3_ref, second3_ref)

    def body(left, right):
        sources = [(before((1, 6, 7)), three[left]), (after((1, 6, 0)), three[right])]
        copies = []
        for t in range(tiles):
            at = pl.ds(t * height, height)
            dproj = near_ref[at, :] + banded(band_ref, t, sources)
            held_ref[at, :] = lax.dot_general(
                dproj.astype(BF16), weight_ref[...], (((1,), (1,)), ((), ())), preferred_element_type=F32
            ).astype(BF16)
            copies.append(pltpu.make_async_copy(held_ref.at[at], out_ref.at[at], sems.at[t]))
            copies[-1].start()
        for copy in copies:
            copy.wait()

    by_parity(body)


def kernel_call(body, ins, outs, cost, specs=None, out_specs=None, **more):
    return pl.pallas_call(
        body,
        out_shape=outs,
        in_specs=specs or [whole()] * len(ins),
        out_specs=out_specs or [whole()] * len(outs),
        compiler_params=pltpu.CompilerParams(vmem_limit_bytes=VMEM_BYTES),
        cost_estimate=pl.CostEstimate(flops=cost, bytes_accessed=0, transcendentals=0),
        **more,
    )(*ins)


def swap_pairs(start, across):
    count, run = lax.axis_size(LINE), lax.axis_size(LINE[1])
    pairs = [(i, i + 1) for i in range(start, count - 1, 2)]
    pairs = [(i, j) for i, j in pairs if across is None or (j % run == 0) == across]
    return pairs + [(j, i) for i, j in pairs]


def swapped(first, second, across=None):
    return [lax.ppermute(x, LINE, swap_pairs(start, across)) for x, start in ((first, 0), (second, 1))]


def partner(j, d, n):
    return j ^ d if n & (n - 1) == 0 else (j + d) % n


def from_all(parts, axis):
    n = lax.axis_size(axis)
    return [
        lax.ppermute(parts(d), axis, [(j, partner(j, d, n)) for j in range(n)]) for d in range(1, n)
    ]


def scatter(x, axis, dtype):
    n = lax.axis_size(axis)
    me = lax.axis_index(axis)
    step = x.shape[0] // n

    def part(d):
        return lax.dynamic_slice_in_dim(x, partner(me, d, n) * step, step)

    return part(0) if n & (n - 1) == 0 else lax.dynamic_slice_in_dim(x, me * step, step), from_all(
        lambda d: part(d).astype(dtype), axis
    )


def add_all(kept, came):
    for part in came:
        kept = kept + part.astype(F32)
    return kept


def pairwise(parts):
    parts = [part.astype(F32) for part in parts]
    while len(parts) > 1:
        parts = [parts[i] + parts[i + 1] for i in range(0, len(parts), 2)]
    return parts[0]


def join_kernel(*refs):
    *parts, out_ref = refs
    n = lax.axis_size(LEVEL[1])
    me = lax.axis_index(LEVEL[1])
    halves = lax.axis_size(LEVEL[0])
    step = parts[0].shape[0] // halves
    for d, part in enumerate(parts):
        origin = me ^ d if n & (n - 1) == 0 else lax.rem(me - d + n, n)
        for h in range(halves):
            first = pl.multiple_of(h * n * step + origin * step, step)
            out_ref[pl.ds(first, step), :] = part[h * step : (h + 1) * step, :].astype(out_ref.dtype)


def term_of(mixed, dagg):
    return lax.dot_general(mixed, dagg, (((0,), (0,)), ((), ())), preferred_element_type=F32)


def shards(feats, weight, cols, vals, cotangent):
    rows, slots = cols.shape[1:]
    size = vals.shape[3]
    width = feats.shape[2]
    zones = rows * size
    tiles = rows // PAIR
    height = PAIR * size
    span = 2 * REACH + PAIR
    own = feats[0]
    product = zones * zones * width

    def chip(blocks, dtype=BF16):
        return pltpu.VMEM((blocks * size, width), dtype)

    def plain(blocks, dtype=BF16):
        return jax.ShapeDtypeStruct((blocks * size, width), dtype)

    cut = kernel_call(
        cut_kernel, [pltpu.with_memory_space_constraint(own, pltpu.HBM)],
        [chip(5), chip(5), chip(2), chip(2)], 0, [anywhere()],
        scratch_shapes=[pltpu.SemaphoreType.DMA((4,))],
    )
    five = swapped(*cut[:2])
    two = swapped(*cut[2:])

    band, near = kernel_call(
        build_kernel, [cols[0], vals[0], own],
        [pltpu.VMEM((tiles, span, height, size), BF16), chip(rows, F32)], 4 * product,
        [pl.BlockSpec(memory_space=pltpu.SMEM), anywhere(), whole()],
        scratch_shapes=[pltpu.SemaphoreType.DMA((rows, slots))],
    )
    band, near = held(band, near)
    mixed_mid, mid = kernel_call(
        inner_kernel, [band, near, *five, weight, cotangent[0]], [chip(4), chip(4)], product
    )
    four = swapped(mid, mid)
    mixed_end, end, *three = kernel_call(
        outer_kernel, [band, near, *five, *two, weight, cotangent[0]],
        [chip(4), chip(4), chip(3), chip(3)], product,
    )
    three = swapped(*three)
    full = [chip(rows, F32)]

    def mark(*given):
        return kernel_call(mark_kernel, held(*given), [pltpu.VMEM((8, 128), F32)], LONG * product)[0]

    term = term_of(mixed_mid, mid) + term_of(mixed_end, end)
    kept, came = scatter(term, LEVEL[0], F32)
    near, activ = kernel_call(
        own_kernel, [band, mid, end, mixed_mid, mixed_end, weight], [*full, plain(rows)], LONG * product
    )
    came, near = lax.optimization_barrier((came, near))
    near = kernel_call(
        functools.partial(add_kernel, (2, 3, 4, 5), (2, 3, 4, 5)), [band, *held(near), *four], full, LONG * product
    )[0]
    kept, came, near = lax.optimization_barrier((kept, came, near))
    kept, came = scatter(add_all(kept, came), LEVEL[1], BF16)
    came, early = lax.optimization_barrier((came, mark(near)))
    term = add_all(kept, came).astype(BF16)
    parts = [term, *from_all(lambda d: term, "rep")]
    *parts, left, right = lax.optimization_barrier((*parts, *three))
    three = [left, right]
    feat_grad = kernel_call(
        back_kernel, [band, *held(near), *three, weight, *held(early)], [plain(rows)], LONG * product,
        out_specs=[anywhere()],
        scratch_shapes=[pltpu.VMEM((zones, width), BF16), pltpu.SemaphoreType.DMA((tiles,))],
    )[0]
    term = pairwise(parts).astype(BF16)
    other, = from_all(lambda d: term, LEVEL[0])
    term = jnp.where(lax.axis_index(LEVEL[0]) == 0, jnp.stack([term, other]), jnp.stack([other, term]))
    term = term.reshape(-1, width)
    parts = [term, *from_all(lambda d: term, LEVEL[1])]
    weight_grad = kernel_call(
        join_kernel, parts, [jax.ShapeDtypeStruct((width, width), F32)], 0
    )[0]
    return activ[None], feat_grad[None], weight_grad


def solution(mesh):
    placed = (
        P("dp", LINE, None),
        P(),
        P("dp", LINE, None),
        P("dp", LINE, None, None, None),
        P("dp", LINE, None),
    )
    return jax.shard_map(
        shards,
        mesh=mesh,
        in_specs=placed,
        out_specs=(P("dp", LINE, None), P("dp", LINE, None), P()),
        check_vma=False,
    )
```

```python
import functools

import jax
import jax.numpy as jnp
from jax import lax
from jax.experimental import pallas as pl
from jax.experimental.pallas import tpu as pltpu
from jax.sharding import PartitionSpec as P

REACH = 7
PAIR = 2
LINE = ("blk", "rep")
LEVEL = ("dp", "blk")
VMEM_BYTES = 14 << 20
LONG = 12
BF16, F32 = jnp.bfloat16, jnp.float32


def whole():
    return pl.BlockSpec(memory_space=pltpu.VMEM)


def anywhere():
    return pl.BlockSpec(memory_space=pl.ANY)


def held(*arrays):
    return [pltpu.with_memory_space_constraint(x, pltpu.VMEM) for x in arrays]


def place():
    return lax.axis_index(LINE[0]) * lax.axis_size(LINE[1]) + lax.axis_index(LINE[1])


def is_odd():
    return lax.rem(place(), 2)


def by_parity(body):
    odd = is_odd()

    @pl.when(odd == 0)
    def _():
        body(1, 0)

    @pl.when(odd == 1)
    def _():
        body(0, 1)


def before(blocks):
    return [b - 1 for b in blocks]


def mine(blocks):
    return [REACH + b for b in blocks]


def after(blocks):
    return [2 * REACH + 1 + b for b in blocks]


def banded(band_ref, t, sources):
    size = band_ref.shape[3]
    left, right = [], []
    for indices, ref in sources:
        for i, w in enumerate(indices):
            if 0 <= w - PAIR * t < band_ref.shape[1]:
                left.append(band_ref[t, w - PAIR * t])
                right.append(ref[i * size : (i + 1) * size, :])
    return jnp.dot(
        jnp.concatenate(left, axis=1), jnp.concatenate(right, axis=0), preferred_element_type=F32
    )


def cut_kernel(feats_ref, *refs):
    outs, sems = refs[:-1], refs[-1]
    size = feats_ref.shape[0] // (REACH + 1)
    odd = is_odd()
    copies = []
    for i, (out, even_first, odd_first) in enumerate(zip(outs, (3, 0, 1, 5), (0, 3, 5, 1))):
        first = jnp.where(odd == 0, even_first, odd_first)
        source = feats_ref.at[pl.ds(pl.multiple_of(first * size, size), out.shape[0])]
        copies.append(pltpu.make_async_copy(source, out, sems.at[i]))
        copies[-1].start()
    for copy in copies:
        copy.wait()


def build_kernel(cols_ref, vals_ref, feats_ref, band_ref, near_ref, sems):
    rows, slots = cols_ref.shape
    tiles, span, height, size = band_ref.shape
    first = place() * rows - REACH

    def clear(i, _):
        band_ref[i // span, i % span] = jnp.zeros((height, size), band_ref.dtype)
        return 0

    lax.fori_loop(0, tiles * span, clear, 0)

    def each(r, act):
        for k in range(slots):
            column = cols_ref[r, k]

            @pl.when(column >= 0)
            def _():
                act(
                    pltpu.make_async_copy(
                        vals_ref.at[r, k],
                        band_ref.at[
                            r // PAIR, column - first - PAIR * (r // PAIR), pl.ds((r % PAIR) * size, size)
                        ],
                        sems.at[r, k],
                    )
                )

    for r in range(rows):
        each(r, lambda copy: copy.start())
    for t in range(tiles):
        for r in range(PAIR * t, PAIR * (t + 1)):
            each(r, lambda copy: copy.wait())
        near_ref[pl.ds(t * height, height), :] = banded(
            band_ref, t, [(mine(range(rows)), feats_ref)]
        )


def tile_step(band_ref, near_ref, sources, t, weight_ref, cot_ref):
    height = band_ref.shape[2]
    at = pl.ds(t * height, height)
    mixed = (near_ref[at, :] + banded(band_ref, t, sources)).astype(BF16)
    agg = jnp.dot(mixed, weight_ref[...], preferred_element_type=F32)
    sig = jax.nn.sigmoid(agg)
    dagg = cot_ref[at, :].astype(F32) * sig * (1.0 + agg * (1.0 - sig))
    return mixed, dagg.astype(BF16)


def inner_kernel(band_ref, near_ref, first5_ref, second5_ref, weight_ref, cot_ref, mixed_ref, mid_ref):
    height = band_ref.shape[2]
    five = (first5_ref, second5_ref)

    def body(left, right):
        sources = [(before(range(3, 8)), five[left]), (after(range(5)), five[right])]
        for i, t in enumerate((1, 2)):
            mixed, dagg = tile_step(band_ref, near_ref, sources, t, weight_ref, cot_ref)
            at = pl.ds(i * height, height)
            mixed_ref[at, :] = mixed
            mid_ref[at, :] = dagg

    by_parity(body)


def outer_kernel(band_ref, near_ref, first5_ref, second5_ref, first2_ref, second2_ref, weight_ref, cot_ref,
                 mixed_ref, end_ref, first3_ref, second3_ref):
    size = band_ref.shape[3]
    height = PAIR * size
    five, two = (first5_ref, second5_ref), (first2_ref, second2_ref)
    three = (first3_ref, second3_ref)

    def body(left, right):
        sources = [
            (before(range(1, 3)), two[left]),
            (before(range(3, 8)), five[left]),
            (after(range(5)), five[right]),
            (after(range(5, 7)), two[right]),
        ]
        mixed, dagg = tile_step(band_ref, near_ref, sources, 0, weight_ref, cot_ref)
        mixed_ref[:height, :] = mixed
        end_ref[:height, :] = dagg
        for out in three:
            out[:size, :] = dagg[size:]
        three[left][2 * size :, :] = dagg[:size]
        mixed, dagg = tile_step(band_ref, near_ref, sources, 3, weight_ref, cot_ref)
        mixed_ref[height:, :] = mixed
        end_ref[height:, :] = dagg
        for out in three:
            out[size : 2 * size, :] = dagg[:size]
        three[right][2 * size :, :] = dagg[size:]

    by_parity(body)


def own_kernel(band_ref, mid_ref, end_ref, mixed_mid_ref, mixed_end_ref, weight_ref, near_ref, activ_ref):
    tiles, _, height, _ = band_ref.shape
    sources = [
        (mine((0, 1)), end_ref.at[:height]),
        (mine((2, 3, 4, 5)), mid_ref),
        (mine((6, 7)), end_ref.at[height:]),
    ]
    halves = (mixed_end_ref[:height, :], mixed_mid_ref[:height, :], mixed_mid_ref[height:, :], mixed_end_ref[height:, :])
    for t, mixed in enumerate(halves):
        at = pl.ds(t * height, height)
        near_ref[at, :] = banded(band_ref, t, sources)
        agg = jnp.dot(mixed, weight_ref[...], preferred_element_type=F32)
        activ_ref[at, :] = (agg * jax.nn.sigmoid(agg)).astype(activ_ref.dtype)


def mark_kernel(near_ref, out_ref):
    out_ref[...] = near_ref[: out_ref.shape[0], : out_ref.shape[1]]


LAST = before((1, 6, 7)) + after((1, 6, 0))


def last_of(t, span):
    return [i for i, w in enumerate(LAST) if 0 <= w - PAIR * t < span]


def add_kernel(left_rows, right_rows, band_ref, near_ref, first_ref, second_ref, out_ref, last_ref):
    tiles, span, height, _ = band_ref.shape
    came = (first_ref, second_ref)
    for t in range(tiles):
        for i, which in enumerate(last_of(t, span)):
            last_ref[t, i] = band_ref[t, LAST[which] - PAIR * t]

    def body(left, right):
        sources = [(before(left_rows), came[left]), (after(right_rows), came[right])]
        for t in range(tiles):
            at = pl.ds(t * height, height)
            out_ref[at, :] = near_ref[at, :] + banded(band_ref, t, sources)

    by_parity(body)


def back_kernel(last_ref, near_ref, first3_ref, second3_ref, weight_ref, _, out_ref, held_ref, sems):
    tiles, _, height, size = last_ref.shape
    three = (first3_ref, second3_ref)

    def body(left, right):
        sources = [(side, i * size) for side in (left, right) for i in range(3)]
        copies = []
        for t in range(tiles):
            at = pl.ds(t * height, height)
            met = last_of(t, 2 * REACH + PAIR)
            blocks = [three[side][first : first + size, :] for side, first in (sources[i] for i in met)]
            dproj = near_ref[at, :] + jnp.dot(
                jnp.concatenate([last_ref[t, i] for i in range(len(met))], axis=1),
                jnp.concatenate(blocks, axis=0),
                preferred_element_type=F32,
            )
            held_ref[at, :] = lax.dot_general(
                dproj.astype(BF16), weight_ref[...], (((1,), (1,)), ((), ())), preferred_element_type=F32
            ).astype(BF16)
            copies.append(pltpu.make_async_copy(held_ref.at[at], out_ref.at[at], sems.at[t]))
            copies[-1].start()
        for copy in copies:
            copy.wait()

    by_parity(body)


def kernel_call(body, ins, outs, cost, specs=None, out_specs=None, **more):
    return pl.pallas_call(
        body,
        out_shape=outs,
        in_specs=specs or [whole()] * len(ins),
        out_specs=out_specs or [whole()] * len(outs),
        compiler_params=pltpu.CompilerParams(vmem_limit_bytes=VMEM_BYTES),
        cost_estimate=pl.CostEstimate(flops=cost, bytes_accessed=0, transcendentals=0),
        **more,
    )(*ins)


def swap_pairs(start, across):
    count, run = lax.axis_size(LINE), lax.axis_size(LINE[1])
    pairs = [(i, i + 1) for i in range(start, count - 1, 2)]
    pairs = [(i, j) for i, j in pairs if across is None or (j % run == 0) == across]
    return pairs + [(j, i) for i, j in pairs]


def swapped(first, second, across=None):
    return [lax.ppermute(x, LINE, swap_pairs(start, across)) for x, start in ((first, 0), (second, 1))]


def partner(j, d, n):
    return j ^ d if n & (n - 1) == 0 else (j + d) % n


def from_all(parts, axis):
    n = lax.axis_size(axis)
    return [
        lax.ppermute(parts(d), axis, [(j, partner(j, d, n)) for j in range(n)]) for d in range(1, n)
    ]


def scatter(x, axis, dtype):
    n = lax.axis_size(axis)
    me = lax.axis_index(axis)
    step = x.shape[0] // n

    def part(d):
        return lax.dynamic_slice_in_dim(x, partner(me, d, n) * step, step)

    return part(0) if n & (n - 1) == 0 else lax.dynamic_slice_in_dim(x, me * step, step), from_all(
        lambda d: part(d).astype(dtype), axis
    )


def add_all(kept, came):
    for part in came:
        kept = kept + part.astype(F32)
    return kept


def pairwise(parts):
    parts = [part.astype(F32) for part in parts]
    while len(parts) > 1:
        parts = [parts[i] + parts[i + 1] for i in range(0, len(parts), 2)]
    return parts[0]


def join_kernel(*refs):
    *parts, out_ref = refs
    n = lax.axis_size(LEVEL[1])
    me = lax.axis_index(LEVEL[1])
    halves = lax.axis_size(LEVEL[0])
    step = parts[0].shape[0] // halves
    for d, part in enumerate(parts):
        origin = me ^ d if n & (n - 1) == 0 else lax.rem(me - d + n, n)
        for h in range(halves):
            first = pl.multiple_of(h * n * step + origin * step, step)
            out_ref[pl.ds(first, step), :] = part[h * step : (h + 1) * step, :].astype(out_ref.dtype)


def term_of(mixed, dagg):
    return lax.dot_general(mixed, dagg, (((0,), (0,)), ((), ())), preferred_element_type=F32)


def shards(feats, weight, cols, vals, cotangent):
    rows, slots = cols.shape[1:]
    size = vals.shape[3]
    width = feats.shape[2]
    zones = rows * size
    tiles = rows // PAIR
    height = PAIR * size
    span = 2 * REACH + PAIR
    own = feats[0]
    product = zones * zones * width

    def chip(blocks, dtype=BF16):
        return pltpu.VMEM((blocks * size, width), dtype)

    def plain(blocks, dtype=BF16):
        return jax.ShapeDtypeStruct((blocks * size, width), dtype)

    cut = kernel_call(
        cut_kernel, [pltpu.with_memory_space_constraint(own, pltpu.HBM)],
        [chip(5), chip(5), chip(2), chip(2)], 0, [anywhere()],
        scratch_shapes=[pltpu.SemaphoreType.DMA((4,))],
    )
    five = swapped(*cut[:2])
    two = swapped(*cut[2:])

    band, near = kernel_call(
        build_kernel, [cols[0], vals[0], own],
        [pltpu.VMEM((tiles, span, height, size), BF16), chip(rows, F32)], 4 * product,
        [pl.BlockSpec(memory_space=pltpu.SMEM), anywhere(), whole()],
        scratch_shapes=[pltpu.SemaphoreType.DMA((rows, slots))],
    )
    band, near = held(band, near)
    mixed_mid, mid = kernel_call(
        inner_kernel, [band, near, *five, weight, cotangent[0]], [chip(4), chip(4)], product
    )
    four = swapped(mid, mid)
    mixed_end, end, *three = kernel_call(
        outer_kernel, [band, near, *five, *two, weight, cotangent[0]],
        [chip(4), chip(4), chip(3), chip(3)], product,
    )
    three = swapped(*three)
    full = [chip(rows, F32)]

    def mark(*given):
        return kernel_call(mark_kernel, held(*given), [pltpu.VMEM((8, 128), F32)], LONG * product)[0]

    term = term_of(mixed_mid, mid) + term_of(mixed_end, end)
    kept, came = scatter(term, LEVEL[0], F32)
    near, activ = kernel_call(
        own_kernel, [band, mid, end, mixed_mid, mixed_end, weight], [*full, plain(rows)], LONG * product
    )
    came, near = lax.optimization_barrier((came, near))
    near, last = kernel_call(
        functools.partial(add_kernel, (2, 3, 4, 5), (2, 3, 4, 5)), [band, *held(near), *four],
        [*full, pltpu.VMEM((tiles, len(last_of(0, span)), height, size), BF16)], LONG * product,
    )
    kept, came, near = lax.optimization_barrier((kept, came, near))
    kept, came = scatter(add_all(kept, came), LEVEL[1], BF16)
    came, early = lax.optimization_barrier((came, mark(near)))
    term = add_all(kept, came).astype(BF16)
    parts = [term, *from_all(lambda d: term, "rep")]
    *parts, left, right = lax.optimization_barrier((*parts, *three))
    three = [left, right]
    feat_grad = kernel_call(
        back_kernel, [*held(last, near), *three, weight, *held(early)], [plain(rows)], LONG * product,
        out_specs=[anywhere()],
        scratch_shapes=[pltpu.VMEM((zones, width), BF16), pltpu.SemaphoreType.DMA((tiles,))],
    )[0]
    term = pairwise(parts).astype(BF16)
    other, = from_all(lambda d: term, LEVEL[0])
    term = jnp.where(lax.axis_index(LEVEL[0]) == 0, jnp.stack([term, other]), jnp.stack([other, term]))
    term = term.reshape(-1, width)
    parts = [term, *from_all(lambda d: term, LEVEL[1])]
    weight_grad = kernel_call(
        join_kernel, parts, [jax.ShapeDtypeStruct((width, width), F32)], 0
    )[0]
    return activ[None], feat_grad[None], weight_grad


def solution(mesh):
    placed = (
        P("dp", LINE, None),
        P(),
        P("dp", LINE, None),
        P("dp", LINE, None, None, None),
        P("dp", LINE, None),
    )
    return jax.shard_map(
        shards,
        mesh=mesh,
        in_specs=placed,
        out_specs=(P("dp", LINE, None), P("dp", LINE, None), P()),
        check_vma=False,
    )
```

```python
import jax
import jax.numpy as jnp
from jax import lax
from jax.experimental import pallas as pl
from jax.experimental.pallas import tpu as pltpu
from jax.sharding import PartitionSpec as P

REACH = 7
PAIR = 2
LINE = ("blk", "rep")
LEVEL = ("dp", "blk")
VMEM_BYTES = 14 << 20
BF16, F32 = jnp.bfloat16, jnp.float32


def whole():
    return pl.BlockSpec(memory_space=pltpu.VMEM)


def anywhere():
    return pl.BlockSpec(memory_space=pl.ANY)


def held(*arrays):
    return [pltpu.with_memory_space_constraint(x, pltpu.VMEM) for x in arrays]


def place():
    return lax.axis_index(LINE[0]) * lax.axis_size(LINE[1]) + lax.axis_index(LINE[1])


def is_odd():
    return lax.rem(place(), 2)


def by_parity(body):
    odd = is_odd()

    @pl.when(odd == 0)
    def _():
        body(1, 0)

    @pl.when(odd == 1)
    def _():
        body(0, 1)


def before(blocks):
    return [b - 1 for b in blocks]


def mine(blocks):
    return [REACH + b for b in blocks]


def after(blocks):
    return [2 * REACH + 1 + b for b in blocks]


def banded(band_ref, t, sources):
    size = band_ref.shape[3]
    left, right = [], []
    for indices, ref in sources:
        for i, w in enumerate(indices):
            if 0 <= w - PAIR * t < band_ref.shape[1]:
                left.append(band_ref[t, w - PAIR * t])
                right.append(ref[i * size : (i + 1) * size, :])
    return jnp.dot(
        jnp.concatenate(left, axis=1), jnp.concatenate(right, axis=0), preferred_element_type=F32
    )


def cut_kernel(feats_ref, *refs):
    outs, sems = refs[:-1], refs[-1]
    size = feats_ref.shape[0] // (REACH + 1)
    odd = is_odd()
    copies = []
    for i, (out, even_first, odd_first) in enumerate(zip(outs, (3, 0, 1, 5), (0, 3, 5, 1))):
        first = jnp.where(odd == 0, even_first, odd_first)
        source = feats_ref.at[pl.ds(pl.multiple_of(first * size, size), out.shape[0])]
        copies.append(pltpu.make_async_copy(source, out, sems.at[i]))
        copies[-1].start()
    for copy in copies:
        copy.wait()


def build_kernel(cols_ref, vals_ref, feats_ref, band_ref, near_ref, sems):
    rows, slots = cols_ref.shape
    tiles, span, height, size = band_ref.shape
    first = place() * rows - REACH

    def clear(i, _):
        band_ref[i // span, i % span] = jnp.zeros((height, size), band_ref.dtype)
        return 0

    lax.fori_loop(0, tiles * span, clear, 0)

    def each(r, act):
        for k in range(slots):
            column = cols_ref[r, k]

            @pl.when(column >= 0)
            def _():
                act(
                    pltpu.make_async_copy(
                        vals_ref.at[r, k],
                        band_ref.at[
                            r // PAIR, column - first - PAIR * (r // PAIR), pl.ds((r % PAIR) * size, size)
                        ],
                        sems.at[r, k],
                    )
                )

    for r in range(rows):
        each(r, lambda copy: copy.start())
    for t in range(tiles):
        for r in range(PAIR * t, PAIR * (t + 1)):
            each(r, lambda copy: copy.wait())
        near_ref[pl.ds(t * height, height), :] = banded(
            band_ref, t, [(mine(range(rows)), feats_ref)]
        )


def tile_step(band_ref, near_ref, sources, t, weight_ref, cot_ref):
    height = band_ref.shape[2]
    at = pl.ds(t * height, height)
    mixed = (near_ref[at, :] + banded(band_ref, t, sources)).astype(BF16)
    agg = jnp.dot(mixed, weight_ref[...], preferred_element_type=F32)
    sig = jax.nn.sigmoid(agg)
    dagg = cot_ref[at, :].astype(F32) * sig * (1.0 + agg * (1.0 - sig))
    return mixed, dagg.astype(BF16)


def inner_kernel(band_ref, near_ref, first5_ref, second5_ref, weight_ref, cot_ref, mixed_ref, mid_ref):
    height = band_ref.shape[2]
    five = (first5_ref, second5_ref)

    def body(left, right):
        sources = [(before(range(3, 8)), five[left]), (after(range(5)), five[right])]
        for i, t in enumerate((1, 2)):
            mixed, dagg = tile_step(band_ref, near_ref, sources, t, weight_ref, cot_ref)
            at = pl.ds(i * height, height)
            mixed_ref[at, :] = mixed
            mid_ref[at, :] = dagg

    by_parity(body)


def outer_kernel(band_ref, near_ref, first5_ref, second5_ref, first2_ref, second2_ref, weight_ref, cot_ref,
                 mixed_ref, end_ref, first3_ref, second3_ref):
    size = band_ref.shape[3]
    height = PAIR * size
    five, two = (first5_ref, second5_ref), (first2_ref, second2_ref)
    three = (first3_ref, second3_ref)

    def body(left, right):
        sources = [
            (before(range(1, 3)), two[left]),
            (before(range(3, 8)), five[left]),
            (after(range(5)), five[right]),
            (after(range(5, 7)), two[right]),
        ]
        mixed, dagg = tile_step(band_ref, near_ref, sources, 0, weight_ref, cot_ref)
        mixed_ref[:height, :] = mixed
        end_ref[:height, :] = dagg
        for out in three:
            out[:size, :] = dagg[size:]
        three[left][2 * size :, :] = dagg[:size]
        mixed, dagg = tile_step(band_ref, near_ref, sources, 3, weight_ref, cot_ref)
        mixed_ref[height:, :] = mixed
        end_ref[height:, :] = dagg
        for out in three:
            out[size : 2 * size, :] = dagg[:size]
        three[right][2 * size :, :] = dagg[size:]

    by_parity(body)


def own_kernel(band_ref, mid_ref, end_ref, mixed_mid_ref, mixed_end_ref, weight_ref, near_ref, activ_ref):
    tiles, _, height, _ = band_ref.shape
    sources = [
        (mine((0, 1)), end_ref.at[:height]),
        (mine((2, 3, 4, 5)), mid_ref),
        (mine((6, 7)), end_ref.at[height:]),
    ]
    halves = (mixed_end_ref[:height, :], mixed_mid_ref[:height, :], mixed_mid_ref[height:, :], mixed_end_ref[height:, :])
    for t, mixed in enumerate(halves):
        at = pl.ds(t * height, height)
        near_ref[at, :] = banded(band_ref, t, sources)
        agg = jnp.dot(mixed, weight_ref[...], preferred_element_type=F32)
        activ_ref[at, :] = (agg * jax.nn.sigmoid(agg)).astype(activ_ref.dtype)


LAST = before((1, 6, 7)) + after((1, 6, 0))


def last_of(t, span):
    return [i for i, w in enumerate(LAST) if 0 <= w - PAIR * t < span]


def add_kernel(band_ref, near_ref, first4_ref, second4_ref, out_ref, last_ref):
    tiles, span, height, _ = band_ref.shape
    for t in range(tiles):
        for i, which in enumerate(last_of(t, span)):
            last_ref[t, i] = band_ref[t, LAST[which] - PAIR * t]
    four = (first4_ref, second4_ref)

    def body(left, right):
        sources = [(before(range(2, 6)), four[left]), (after(range(2, 6)), four[right])]
        for t in range(tiles):
            at = pl.ds(t * height, height)
            out_ref[at, :] = near_ref[at, :] + banded(band_ref, t, sources)

    by_parity(body)


def back_kernel(last_ref, near_ref, first3_ref, second3_ref, weight_ref, out_ref, held_ref, sems):
    tiles, _, height, size = last_ref.shape
    three = (first3_ref, second3_ref)

    def body(left, right):
        sources = [(side, i * size) for side in (left, right) for i in range(3)]
        copies = []
        for t in range(tiles):
            at = pl.ds(t * height, height)
            met = last_of(t, 2 * REACH + PAIR)
            blocks = [three[side][first : first + size, :] for side, first in (sources[i] for i in met)]
            dproj = near_ref[at, :] + jnp.dot(
                jnp.concatenate([last_ref[t, i] for i in range(len(met))], axis=1),
                jnp.concatenate(blocks, axis=0),
                preferred_element_type=F32,
            )
            held_ref[at, :] = lax.dot_general(
                dproj.astype(BF16), weight_ref[...], (((1,), (1,)), ((), ())), preferred_element_type=F32
            ).astype(BF16)
            copies.append(pltpu.make_async_copy(held_ref.at[at], out_ref.at[at], sems.at[t]))
            copies[-1].start()
        for copy in copies:
            copy.wait()

    by_parity(body)


def kernel_call(body, ins, outs, cost, specs=None, out_specs=None, **more):
    return pl.pallas_call(
        body,
        out_shape=outs,
        in_specs=specs or [whole()] * len(ins),
        out_specs=out_specs or [whole()] * len(outs),
        compiler_params=pltpu.CompilerParams(vmem_limit_bytes=VMEM_BYTES),
        cost_estimate=pl.CostEstimate(flops=cost, bytes_accessed=0, transcendentals=0),
        **more,
    )(*ins)


def swapped(first, second):
    count = lax.axis_size(LINE)
    result = []
    for x, start in ((first, 0), (second, 1)):
        pairs = [(i, i + 1) for i in range(start, count - 1, 2)]
        result.append(lax.ppermute(x, LINE, pairs + [(j, i) for i, j in pairs]))
    return result


def partner(j, d, n):
    return j ^ d if n & (n - 1) == 0 else (j + d) % n


def from_all(parts, axis):
    n = lax.axis_size(axis)
    return [
        lax.ppermute(parts(d), axis, [(j, partner(j, d, n)) for j in range(n)]) for d in range(1, n)
    ]


def pairwise(parts):
    parts = [part.astype(F32) for part in parts]
    while len(parts) > 1:
        parts = [parts[i] + parts[i + 1] for i in range(0, len(parts), 2)]
    return parts[0]


def join_kernel(*refs):
    *parts, out_ref = refs
    n = lax.axis_size(LEVEL[1])
    me = lax.axis_index(LEVEL[1])
    halves = lax.axis_size(LEVEL[0])
    step = parts[0].shape[0] // halves
    for d, part in enumerate(parts):
        origin = me ^ d if n & (n - 1) == 0 else lax.rem(me - d + n, n)
        for h in range(halves):
            first = pl.multiple_of(h * n * step + origin * step, step)
            out_ref[pl.ds(first, step), :] = part[h * step : (h + 1) * step, :].astype(out_ref.dtype)


def term_of(mixed, dagg):
    return lax.dot_general(mixed, dagg, (((0,), (0,)), ((), ())), preferred_element_type=F32)


def shards(feats, weight, cols, vals, cotangent):
    rows, slots = cols.shape[1:]
    size = vals.shape[3]
    width = feats.shape[2]
    zones = rows * size
    tiles = rows // PAIR
    height = PAIR * size
    span = 2 * REACH + PAIR
    own = feats[0]
    product = zones * zones * width

    def chip(blocks, dtype=BF16):
        return pltpu.VMEM((blocks * size, width), dtype)

    def plain(blocks, dtype=BF16):
        return jax.ShapeDtypeStruct((blocks * size, width), dtype)

    cut = kernel_call(
        cut_kernel, [pltpu.with_memory_space_constraint(own, pltpu.HBM)],
        [chip(5), chip(5), chip(2), chip(2)], 0, [anywhere()],
        scratch_shapes=[pltpu.SemaphoreType.DMA((4,))],
    )
    five = swapped(*cut[:2])
    two = swapped(*cut[2:])

    band, near = kernel_call(
        build_kernel, [cols[0], vals[0], own],
        [pltpu.VMEM((tiles, span, height, size), BF16), chip(rows, F32)], 4 * product,
        [pl.BlockSpec(memory_space=pltpu.SMEM), anywhere(), whole()],
        scratch_shapes=[pltpu.SemaphoreType.DMA((rows, slots))],
    )
    band, near = held(band, near)
    mixed_mid, mid = kernel_call(
        inner_kernel, [band, near, *five, weight, cotangent[0]], [chip(4), chip(4)], product
    )
    four = swapped(mid, mid)
    mixed_end, end, *sent = kernel_call(
        outer_kernel, [band, near, *five, *two, weight, cotangent[0]],
        [chip(4), chip(4), chip(3), chip(3)], product,
    )
    three = swapped(*sent)
    near, activ = kernel_call(
        own_kernel, [band, mid, end, mixed_mid, mixed_end, weight], [chip(rows, F32), plain(rows)], product
    )
    near, last = kernel_call(
        add_kernel, [band, held(near)[0], *four],
        [chip(rows, F32), pltpu.VMEM((tiles, len(last_of(0, span)), height, size), BF16)], 12 * product,
    )
    term = term_of(mixed_mid, mid) + term_of(mixed_end, end)
    term = lax.all_to_all(
        term.astype(BF16).reshape(lax.axis_size(LEVEL), -1, width), LEVEL, 0, 0, tiled=True
    )
    term, near = lax.optimization_barrier((term, near))
    term = jnp.sum(term.astype(F32), axis=0)
    term = term.astype(BF16)
    parts = [term, *from_all(lambda d: term, "rep")]
    parts, three = lax.optimization_barrier((parts, three))
    feat_grad = kernel_call(
        back_kernel, [*held(last, near), *three, weight], [plain(rows)], 12 * product,
        out_specs=[anywhere()],
        scratch_shapes=[pltpu.VMEM((zones, width), BF16), pltpu.SemaphoreType.DMA((tiles,))],
    )[0]
    term = pairwise(parts).astype(BF16)
    other, = from_all(lambda d: term, LEVEL[0])
    term = jnp.where(lax.axis_index(LEVEL[0]) == 0, jnp.stack([term, other]), jnp.stack([other, term]))
    term = term.reshape(-1, width)
    parts = [term, *from_all(lambda d: term, LEVEL[1])]
    weight_grad = kernel_call(
        join_kernel, parts, [jax.ShapeDtypeStruct((width, width), F32)], 0
    )[0]
    return activ[None], feat_grad[None], weight_grad


def solution(mesh):
    placed = (
        P("dp", LINE, None),
        P(),
        P("dp", LINE, None),
        P("dp", LINE, None, None, None),
        P("dp", LINE, None),
    )
    return jax.shard_map(
        shards,
        mesh=mesh,
        in_specs=placed,
        out_specs=(P("dp", LINE, None), P("dp", LINE, None), P()),
        check_vma=False,
    )
```
